512 devices in a mesh: row: 64 (over x, z), col: 8 (over y, core).
Axes of the slice: x: 4, y: 4, z: 16, core: 2. Of those that a mesh axis runs over, the one named last changes fastest.
Arguments:
- inverse_kernel: float32 [8192, 8192], P('row', 'col'), as said below
- points: bfloat16 [8192, 1024], P('row', 'col')
- candidates: bfloat16 [1024, 1024], P(None, 'col')
- obs_embed: float32 [8192], P('row'), may hold values from 0.5 to 5
- cand_embed: float32 [1024], replicated, may hold values from 0.05 to 0.5
- chosen: int32 [64], replicated, may hold values from 0 to 1023, as said below
Outputs:
- inverse_update: float32 [8192, 8192], P('row', 'col')
- schur_inverse: float32 [64, 64], replicated
- new_weights: float32 [64], replicated
- weight_shift: float32 [8192], P('row')
The draws below stay inside these ranges and needn't reach their ends.
Inputs may be any that keep to these rules, and one draw needn't show every extreme that they name: inverse_kernel is symmetric. `chosen`: the indices are distinct.
All inputs are finite; a program needn't handle non-finite values.
Results may differ from the reference program's by a relative error of at most 0.0003.
Values sent between devices are 32-bit elements; how exact they have to be, the bound alone decides.
A program may use at most 64 MiB of HBM per device.

```python
import math
import jax
import jax.numpy as jnp
from jax import lax

F = 1024
NEW = 64
CAND = 1024
NOBS = 8192


def draw_cloud(key, count):
    scale_key, base_key = jax.random.split(key)
    scale = jnp.exp(jax.random.uniform(scale_key, (count, 1), jnp.float32, -0.7, 0.7))
    base = jax.random.normal(base_key, (count, F), jnp.float32)
    return (base * scale * (1.0 / math.sqrt(F))).astype(jnp.bfloat16)


def draw_points(key, part):
    return draw_cloud(jax.random.fold_in(key, 11), NOBS)


def draw_candidates(key, part):
    return draw_cloud(jax.random.fold_in(key, 23), CAND)


def draw_inverse_kernel(key, part):
    off_key, diag_key = jax.random.split(jax.random.fold_in(key, 37))
    spread = jax.random.uniform(off_key, (NOBS, NOBS), jnp.float32, -12.0, 12.0)
    symmetric = (spread + spread.T) * 0.5
    diag = jax.random.uniform(diag_key, (NOBS,), jnp.float32, 12.8, 25.6) * NOBS
    eye_mask = jnp.eye(NOBS, dtype=jnp.float32)
    return symmetric * (1.0 - eye_mask) + eye_mask * diag[:, None]


def draw_chosen(key, part):
    return jax.random.permutation(jax.random.fold_in(key, 53), CAND)[:NEW].astype(jnp.int32)


def levels(stream_key, extent, cuts, least, largest):
    def one(position, parts):
        steps = jax.random.uniform(jax.random.fold_in(jax.random.fold_in(stream_key, 6), position), (parts,), jnp.float32, least / len(cuts), largest / len(cuts))
        return jnp.repeat(jnp.exp(steps), extent[position] // parts).reshape((-1,) + (1,) * (len(extent) - position - 1))

    factor_of = one(*cuts[0])
    for cut in cuts[1:]:
        factor_of = factor_of * one(*cut)
    return factor_of


def setup_inputs(seed: int = 0) -> dict:
    streams_of = jax.random.split(jax.random.key(seed), 7)
    return {
        "inverse_kernel": draw_inverse_kernel(jax.random.fold_in(streams_of[6], 71), 0),
        "points": draw_points(jax.random.fold_in(streams_of[6], 71), 0),
        "candidates": draw_candidates(jax.random.fold_in(streams_of[6], 71), 0),
        "obs_embed": jnp.clip(0.5 + 4.5 * jax.random.uniform(streams_of[3], (NOBS,), jnp.float32) ** levels(streams_of[3], (NOBS,), ((0, 64),), -0.2, 0.2), 0.5, 5.0),
        "cand_embed": jnp.clip(jnp.exp(jax.random.uniform(streams_of[4], (CAND,), jnp.float32, math.log(0.05), math.log(0.5))), 0.05, 0.5),
        "chosen": draw_chosen(jax.random.fold_in(streams_of[6], 71), 0),
    }


def matern(square):
    scaled = jnp.sqrt(5.0 * jnp.maximum(square, 0.0))
    return (1.0 + scaled + scaled * scaled / 3.0) * jnp.exp(-scaled)

def reference(inverse_kernel, points, candidates, obs_embed, cand_embed, chosen):
    high = lax.Precision.HIGHEST
    appended = jnp.take(candidates, chosen, axis=0)
    new_embed = jnp.take(cand_embed, chosen, axis=0)
    cross = jnp.dot(points.astype(jnp.float32), appended.T.astype(jnp.float32), preferred_element_type=jnp.float32)
    wide = points.astype(jnp.float32)
    sq_obs = lax.optimization_barrier(jnp.sum(wide * wide, axis=1))
    pair = jnp.dot(appended.astype(jnp.float32), appended.T.astype(jnp.float32), preferred_element_type=jnp.float32)
    sq_new = jnp.diagonal(pair)
    kvec = matern(sq_obs[:, None] + sq_new[None, :] - 2.0 * cross) * (1.0 / (18.0 * NOBS))
    gram = matern(sq_new[:, None] + sq_new[None, :] - 2.0 * pair)
    solved = jnp.dot(inverse_kernel, kvec, precision=high)
    schur = jnp.eye(NEW, dtype=jnp.float32) + gram / NEW - jnp.dot(kvec.T, solved, precision=high)
    quad = jnp.dot(obs_embed, solved, precision=high) / NOBS - new_embed
    factor = jnp.linalg.cholesky(schur)
    schur_inverse = jax.scipy.linalg.cho_solve((factor, True), jnp.eye(NEW, dtype=jnp.float32))
    new_weights = jnp.dot(schur_inverse, quad, precision=high)
    weight_shift = jnp.dot(solved, new_weights, precision=high)
    left = jnp.dot(solved, schur_inverse, precision=high)
    inverse_update = jnp.dot(left, solved.T, precision=high)
    return (inverse_update, schur_inverse, new_weights, weight_shift)
```

```python
import jax
import jax.numpy as jnp
from jax import lax
from jax.experimental import pallas as pl
from jax.experimental.pallas import tpu as pltpu
from jax.sharding import PartitionSpec as P

MESH = pl.DeviceIdType.MESH
HIGH = lax.Precision.HIGHEST
NX, NY, NZ, NC = 4, 4, 16, 2
NOBS = 8192
NEW = 64


def matern(square):
    scaled = jnp.sqrt(5.0 * jnp.maximum(square, 0.0))
    return (1.0 + scaled + scaled * scaled / 3.0) * jnp.exp(-scaled)


def dot_t(a, b, precision=None):
    return lax.dot_general(
        a, b, (((1,), (1,)), ((), ())), precision=precision, preferred_element_type=jnp.float32
    )


def exchange_kernel(
    inv_hbm, points_ref, cand_ref, embed_ref, chosen_ref,
    total_ref, solved_cols_ref, solved_rows_ref,
    inv, a2a_src, a2a_rcv, tile, full, gsrc, grcv, etr, ebuf, srow, fsrc, frcv,
    ss_a, rs_a, ss_z, rs_z, ss_x, rs_x, ss_g, rs_g, ss_r, rs_r, ss_f, rs_f, ss_e, rs_e, ss_ez, rs_ez, inv_sem,
):
    row = lax.axis_index("row")
    col = lax.axis_index("col")
    x, z = row // NZ, row % NZ
    y, core = col // NC, col % NC
    half = z // 8
    spot = z % 8
    mine = 2 * x + core
    on_diag = x == y
    home = core == half

    def send(src, dst, ssem, rsem, to_row, to_col, is_self):
        remote = pltpu.make_async_remote_copy(
            src_ref=src, dst_ref=dst, send_sem=ssem, recv_sem=rsem,
            device_id=(to_row, to_col), device_id_type=MESH,
        )

        @pl.when(is_self)
        def _():
            pltpu.make_async_copy(src, dst, rsem).start()

        @pl.when(jnp.logical_not(is_self))
        def _():
            remote.start()

    def wait_sent(src, dst, ssem, rsem, to_row, to_col, is_self):
        @pl.when(jnp.logical_not(is_self))
        def _():
            pltpu.make_async_remote_copy(
                src_ref=src, dst_ref=dst, send_sem=ssem, recv_sem=rsem,
                device_id=(to_row, to_col), device_id_type=MESH,
            ).wait_send()

    def arrived(dst, rsem):
        pltpu.make_async_copy(dst, dst, rsem).wait()

    inv_copy = pltpu.make_async_copy(inv_hbm, inv, inv_sem)
    inv_copy.start()

    barrier = pltpu.get_barrier_semaphore()

    def greet(to_row, to_col, is_self):
        @pl.when(jnp.logical_not(is_self))
        def _():
            pl.semaphore_signal(barrier, inc=1, device_id=(to_row, to_col), device_id_type=MESH)

    for k in range(8):
        greet(y * NZ + z, jnp.int32(k), jnp.logical_and(on_diag, col == k))
        greet((k // 2) * NZ + z, x * NC + k % 2, jnp.logical_and(on_diag, mine == k))
        greet(row, jnp.int32(k), col == k)
    for k in range(16):
        greet(x * NZ + core * 8 + k // 2, y * NC + k % 2, jnp.logical_and(row % NZ == core * 8 + k // 2, core == k % 2))
    for k in range(4):
        greet(k * NZ + z, col, x == k)

    onehot = (chosen_ref[...] == lax.broadcasted_iota(jnp.int32, (NEW, cand_ref.shape[0]), 1))
    onehot = jnp.where(onehot, 1.0, 0.0).astype(jnp.bfloat16)
    appended = jnp.dot(onehot, cand_ref[...], preferred_element_type=jnp.float32).astype(jnp.bfloat16)
    pts = points_ref[...]
    wide = pts.astype(jnp.float32)
    sq_obs = dot_t(jnp.ones((8, wide.shape[1]), jnp.float32), wide * wide, HIGH)[0:1]
    pair = dot_t(appended, appended)
    eye = lax.broadcasted_iota(jnp.int32, (NEW, NEW), 0) == lax.broadcasted_iota(jnp.int32, (NEW, NEW), 1)
    diagonal = jnp.where(eye, pair, 0.0)
    sq_col = jnp.sum(diagonal, axis=1, keepdims=True)
    sq_row = jnp.sum(diagonal, axis=0, keepdims=True)
    a2a_src[0] = sq_obs + sq_col - 2.0 * dot_t(appended, pts)
    gsrc[:, 0:NEW] = sq_row + sq_col - 2.0 * pair
    gsrc[:, NEW:] = jnp.zeros((NEW, NEW), jnp.float32)

    pl.semaphore_wait(barrier, 41 - 2 * on_diag.astype(jnp.int32) - home.astype(jnp.int32) + 1)

    def a2a_args(p, e):
        return (
            a2a_src.at[p, pl.ds(8 * e, 8)], a2a_rcv.at[p, col], ss_a.at[p, e], rs_a.at[p, col],
            (e // 2) * NZ + z, x * NC + e % 2, jnp.logical_and(on_diag, mine == e),
        )

    def g_args(k):
        return (gsrc.at[pl.ds(8 * k, 8)], grcv.at[col], ss_g.at[k], rs_g.at[col], row, jnp.int32(k), col == k)

    def z_args(p, k):
        return (
            tile.at[p], full.at[p, x, core, spot], ss_z.at[p, k], rs_z.at[p, core, spot],
            x * NZ + k, y * NC + half, jnp.logical_and(home, z == k),
        )

    def x_args(p, k):
        return (full.at[p, x], full.at[p, x], ss_x.at[p, k], rs_x.at[p, x], k * NZ + z, col)

    def e_args():
        return (embed_ref, etr, ss_e, rs_e, y * NZ + z, x * NC + core, on_diag)

    def ez_args(k):
        return (etr, ebuf.at[spot], ss_ez.at[k], rs_ez.at[spot], x * NZ + k, y * NC + half, z == k)

    def r_args(k):
        return (
            tile.at[1], srow.at[mine], ss_r.at[k], rs_r.at[mine],
            y * NZ + z, jnp.int32(k), jnp.logical_and(on_diag, col == k),
        )

    def f_args(k):
        return (fsrc, frcv.at[col], ss_f.at[k], rs_f.at[col], row, jnp.int32(k), col == k)

    def reduce_tiles(p):
        for e in range(8):
            send(*a2a_args(p, e))

    def reduced(p):
        for k in range(8):
            arrived(a2a_rcv.at[p, k], rs_a.at[p, k])
        value = a2a_rcv[p, 0]
        for k in range(1, 8):
            value = value + a2a_rcv[p, k]
        return value

    def spread_z(p):
        for k in range(NZ):
            send(*z_args(p, k))

    def spread_x(p):
        for c in range(NC):
            for s in range(8):
                arrived(full.at[p, x, c, s], rs_z.at[p, c, s])
        for k in range(NX):
            src, dst, ssem, rsem, to_row, to_col = x_args(p, k)

            @pl.when(x != k)
            def _():
                pltpu.make_async_remote_copy(
                    src_ref=src, dst_ref=dst, send_sem=ssem, recv_sem=rsem,
                    device_id=(to_row, to_col), device_id_type=MESH,
                ).start()

    def spread_done(p):
        for k in range(NX):
            @pl.when(x != k)
            def _():
                arrived(full.at[p, k], rs_x.at[p, k])
        parts = [full[p, :, :, s].reshape(NEW, 128) for s in range(8)]
        return jnp.concatenate(parts, axis=1)

    reduce_tiles(0)
    send(*e_args())
    for k in range(8):
        send(*g_args(k))

    tile[0] = matern(reduced(0)) * (1.0 / (18.0 * NOBS))
    spread_z(0)

    arrived(etr, rs_e)

    @pl.when(home)
    def _():
        for k in range(NZ):
            send(*ez_args(k))

    for k in range(8):
        arrived(grcv.at[k], rs_g.at[k])
    gram = grcv[0]
    for k in range(1, 8):
        gram = gram + grcv[k]
    gram = matern(gram[:, 0:NEW]) * (1.0 / NEW)

    spread_x(0)
    kernel_cols = spread_done(0)
    inv_copy.wait()
    a2a_src[1] = dot_t(kernel_cols, inv[...], HIGH)
    reduce_tiles(1)
    tile[1] = reduced(1)
    spread_z(1)
    for k in range(8):
        send(*r_args(k))
    spread_x(1)
    solved_cols = spread_done(1)
    for s in range(8):
        arrived(ebuf.at[s], rs_ez.at[s])
    embed = jnp.concatenate([ebuf[s] for s in range(8)], axis=1)
    fsrc[:, 0:NEW] = -dot_t(solved_cols, kernel_cols, HIGH)
    fsrc[:, NEW:] = jnp.broadcast_to(jnp.sum(solved_cols * embed, axis=1, keepdims=True), (NEW, NEW))
    slot = pl.ds(pl.multiple_of(8 * col, 8), 8)
    fsrc[slot, 0:NEW] = fsrc[slot, 0:NEW] + gram
    for k in range(8):
        send(*f_args(k))
    solved_cols_ref[...] = solved_cols
    for k in range(8):
        arrived(srow.at[k], rs_r.at[k])
    solved_rows_ref[...] = srow[...].reshape(NEW, 128)
    for k in range(8):
        arrived(frcv.at[k], rs_f.at[k])
    total = frcv[0]
    for k in range(1, 8):
        total = total + frcv[k]
    total_ref[...] = total

    wait_sent(*e_args())
    for p in range(2):
        for k in range(8):
            wait_sent(*a2a_args(p, k))
        for k in range(NZ):
            wait_sent(*z_args(p, k))
        for k in range(NX):
            wait_sent(*x_args(p, k), x == k)
    for k in range(8):
        wait_sent(*g_args(k))
        wait_sent(*r_args(k))
        wait_sent(*f_args(k))

    @pl.when(home)
    def _():
        for k in range(NZ):
            wait_sent(*ez_args(k))


def finish_kernel(
    total_ref, solved_cols_ref, solved_rows_ref, chosen_ref, cand_embed_ref,
    update_ref, inverse_ref, weights_ref, shift_ref,
):
    total = total_ref[...]
    sub = lax.broadcasted_iota(jnp.int32, (NEW, NEW), 0)
    lane = lax.broadcasted_iota(jnp.int32, (NEW, NEW), 1)
    matrix = total[:, 0:NEW] + jnp.where(sub == lane, 1.0, 0.0)
    picked = chosen_ref[...] == lax.broadcasted_iota(jnp.int32, (NEW, cand_embed_ref.shape[1]), 1)
    new_embed = jnp.sum(jnp.where(picked, cand_embed_ref[...], 0.0), axis=1, keepdims=True)
    quad = total[:, NEW:NEW + 1] * (1.0 / NOBS) - new_embed
    for k in range(NEW):
        pivot = matrix[k:k + 1, k:k + 1]
        scale = jnp.where(pivot > 0.0, 1.0 / pivot, jnp.nan)
        at_lane = lane == k
        pivot_row = jnp.where(at_lane[0:1], 1.0, matrix[k:k + 1, :]) * scale
        rest = jnp.where(at_lane, 0.0, matrix) - matrix[:, k:k + 1] * pivot_row
        matrix = jnp.where(sub == k, pivot_row, rest)
    inverse_ref[...] = matrix
    weights = jnp.sum(matrix * quad, axis=0, keepdims=True)
    weights_ref[...] = weights
    solved_rows = solved_rows_ref[...]
    shift_ref[...] = jnp.dot(
        jnp.broadcast_to(weights, (8, NEW)), solved_rows, precision=HIGH, preferred_element_type=jnp.float32
    )[0:1]
    left = jnp.dot(matrix, solved_rows, precision=HIGH, preferred_element_type=jnp.float32)
    update_ref[...] = lax.dot_general(
        left, solved_cols_ref[...], (((0,), (0,)), ((), ())), precision=HIGH, preferred_element_type=jnp.float32
    )


def on_device(inverse_kernel, points, candidates, obs_embed, cand_embed, chosen):
    rows, cols = inverse_kernel.shape
    f32 = jnp.float32
    vmem = pl.BlockSpec(memory_space=pltpu.VMEM)
    dma = pltpu.SemaphoreType.DMA
    chosen_col = chosen.reshape(NEW, 1)
    total, solved_cols, solved_rows = pl.pallas_call(
        exchange_kernel,
        out_shape=(
            jax.ShapeDtypeStruct((NEW, 128), f32),
            jax.ShapeDtypeStruct((NEW, cols), f32),
            jax.ShapeDtypeStruct((NEW, rows), f32),
        ),
        in_specs=[pl.BlockSpec(memory_space=pl.ANY), vmem, vmem, vmem, vmem],
        out_specs=(vmem, vmem, vmem),
        scratch_shapes=[
            pltpu.VMEM((rows, cols), f32),
            pltpu.VMEM((2, NEW, 128), f32),
            pltpu.VMEM((2, 8, 8, 128), f32),
            pltpu.VMEM((2, 8, 128), f32),
            pltpu.VMEM((2, NX, NC, 8, 8, 128), f32),
            pltpu.VMEM((NEW, 128), f32),
            pltpu.VMEM((8, 8, 128), f32),
            pltpu.VMEM((1, 128), f32),
            pltpu.VMEM((8, 1, 128), f32),
            pltpu.VMEM((8, 8, 128), f32),
            pltpu.VMEM((NEW, 128), f32),
            pltpu.VMEM((8, NEW, 128), f32),
            dma((2, 8)), dma((2, 8)),
            dma((2, NZ)), dma((2, NC, 8)),
            dma((2, NX)), dma((2, NX)),
            dma((8,)), dma((8,)),
            dma((8,)), dma((8,)),
            dma((8,)), dma((8,)),
            dma, dma,
            dma((NZ,)), dma((8,)),
            dma,
        ],
        compiler_params=pltpu.CompilerParams(collective_id=0, has_side_effects=True),
    )(inverse_kernel, points, candidates, obs_embed.reshape(1, rows), chosen_col)
    update, inverse, weights, shift = pl.pallas_call(
        finish_kernel,
        out_shape=(
            jax.ShapeDtypeStruct((rows, cols), f32),
            jax.ShapeDtypeStruct((NEW, NEW), f32),
            jax.ShapeDtypeStruct((1, NEW), f32),
            jax.ShapeDtypeStruct((1, rows), f32),
        ),
        in_specs=[vmem] * 5,
        out_specs=(vmem,) * 4,
    )(total, solved_cols, solved_rows, chosen_col, cand_embed.reshape(1, -1))
    return update, inverse, weights.reshape(NEW), shift.reshape(rows)


def solution(mesh):
    return jax.shard_map(
        on_device,
        mesh=mesh,
        in_specs=(P("row", "col"), P("row", "col"), P(None, "col"), P("row"), P(), P()),
        out_specs=(P("row", "col"), P(), P(), P("row")),
        check_vma=False,
    )
```

```python
import jax
import jax.numpy as jnp
from jax import lax
from jax.experimental import pallas as pl
from jax.experimental.pallas import tpu as pltpu
from jax.sharding import PartitionSpec as P

MESH = pl.DeviceIdType.MESH
HIGH = lax.Precision.HIGHEST
NX, NY, NZ, NC = 4, 4, 16, 2
NOBS = 8192
NEW = 64
HALF = NEW // 2
FAR = (8, 7, -7, 6, -6, 5, -5, 4, -4, 3, -3, 2, -2, 1, -1, 0)
GROUP = 4


def matern(square):
    scaled = jnp.sqrt(5.0 * jnp.maximum(square, 0.0))
    return (1.0 + scaled + scaled * scaled / 3.0) * jnp.exp(-scaled)


def dot_t(a, b, precision=None):
    return lax.dot_general(
        a, b, (((1,), (1,)), ((), ())), precision=precision, preferred_element_type=jnp.float32
    )


def exchange_kernel(
    inv_hbm, points_ref, cand_ref, embed_ref, chosen_ref, cand_embed_ref,
    total_ref, solved_cols_ref, solved_rows_ref,
    inv, a2a_src, a2a_rcv, tile, full, gsrc, grcv, etr, ebuf, srow, fsrc, frcv,
    ss_a, rs_a, ss_z, rs_z, ss_x, rs_x, ss_g, rs_g, ss_r, rs_r, ss_f, rs_f, ss_e, rs_e, ss_ez, rs_ez, inv_sem,
):
    row = lax.axis_index("row")
    col = lax.axis_index("col")
    x, z = row // NZ, row % NZ
    y, core = col // NC, col % NC
    half = z // 8
    spot = z % 8
    mine = 2 * x + core
    on_diag = x == y
    home = core == half

    def send(src, dst, ssem, rsem, to_row, to_col, is_self):
        remote = pltpu.make_async_remote_copy(
            src_ref=src, dst_ref=dst, send_sem=ssem, recv_sem=rsem,
            device_id=(to_row, to_col), device_id_type=MESH,
        )

        @pl.when(is_self)
        def _():
            pltpu.make_async_copy(src, dst, rsem).start()

        @pl.when(jnp.logical_not(is_self))
        def _():
            remote.start()

    def wait_sent(src, dst, ssem, rsem, to_row, to_col, is_self):
        @pl.when(jnp.logical_not(is_self))
        def _():
            pltpu.make_async_remote_copy(
                src_ref=src, dst_ref=dst, send_sem=ssem, recv_sem=rsem,
                device_id=(to_row, to_col), device_id_type=MESH,
            ).wait_send()

    def arrived(dst, rsem):
        pltpu.make_async_copy(dst, dst, rsem).wait()

    inv_copy = pltpu.make_async_copy(inv_hbm, inv, inv_sem)
    inv_copy.start()

    barrier = pltpu.get_barrier_semaphore()

    def greet(to_row, to_col, is_self):
        @pl.when(jnp.logical_not(is_self))
        def _():
            pl.semaphore_signal(barrier, inc=1, device_id=(to_row, to_col), device_id_type=MESH)

    for k in range(8):
        greet(y * NZ + z, jnp.int32(k), jnp.logical_and(on_diag, col == k))
        greet((k // 2) * NZ + z, x * NC + k % 2, jnp.logical_and(on_diag, mine == k))
        greet(row, jnp.int32(k), col == k)
    for k in range(16):
        greet(x * NZ + core * 8 + k // 2, y * NC + k % 2, jnp.logical_and(row % NZ == core * 8 + k // 2, core == k % 2))
    for k in range(4):
        greet(k * NZ + z, col, x == k)

    onehot = (chosen_ref[...] == lax.broadcasted_iota(jnp.int32, (cand_ref.shape[0], NEW), 0))
    onehot = jnp.where(onehot, 1.0, 0.0)
    appended = lax.dot_general(
        onehot.astype(jnp.bfloat16), cand_ref[...], (((0,), (0,)), ((), ())), preferred_element_type=jnp.float32
    ).astype(jnp.bfloat16)
    pts = points_ref[...]
    wide = pts.astype(jnp.float32)
    sq_obs = dot_t(jnp.ones((8, wide.shape[1]), jnp.float32), wide * wide, HIGH)[0:1]
    pair = dot_t(appended, appended)
    eye = lax.broadcasted_iota(jnp.int32, (NEW, NEW), 0) == lax.broadcasted_iota(jnp.int32, (NEW, NEW), 1)
    diagonal = jnp.where(eye, pair, 0.0)
    sq_col = jnp.sum(diagonal, axis=1, keepdims=True)
    sq_row = jnp.sum(diagonal, axis=0, keepdims=True)
    a2a_src[0] = sq_obs + sq_col - 2.0 * dot_t(appended, pts)
    gsrc[:, 0:NEW] = sq_row + sq_col - 2.0 * pair
    gsrc[:, NEW:] = jnp.zeros((NEW, NEW), jnp.float32)
    fsrc[HALF:, NEW:] = jnp.zeros((8, NEW), jnp.float32)

    pl.semaphore_wait(barrier, 41 - 2 * on_diag.astype(jnp.int32) - home.astype(jnp.int32) + 1)

    def a2a_args(p, e):
        return (
            a2a_src.at[p, pl.ds(8 * e, 8)], a2a_rcv.at[p, col], ss_a.at[p, e], rs_a.at[p, col],
            (e // 2) * NZ + z, x * NC + e % 2, jnp.logical_and(on_diag, mine == e),
        )

    def g_args(k):
        return (gsrc.at[pl.ds(8 * k, 8)], grcv.at[col], ss_g.at[k], rs_g.at[col], row, jnp.int32(k), col == k)

    def z_args(p, k):
        return (
            tile.at[p], full.at[p, x, spot, core], ss_z.at[p, k], rs_z.at[p, spot, core],
            x * NZ + (z + FAR[k]) % NZ, y * NC + half, jnp.logical_and(home, FAR[k] == 0),
        )

    def x_copy(p, k, s):
        return pltpu.make_async_remote_copy(
            src_ref=full.at[p, x, s], dst_ref=full.at[p, x, s], send_sem=ss_x.at[p, k, s], recv_sem=rs_x.at[p, x, s],
            device_id=(((x + k) % NX) * NZ + z, col), device_id_type=MESH,
        )

    def e_args():
        return (embed_ref, etr, ss_e, rs_e, y * NZ + z, x * NC + core, on_diag)

    def ez_args(k):
        return (etr, ebuf.at[spot], ss_ez.at[k], rs_ez.at[spot], x * NZ + k, y * NC + half, z == k)

    def r_args(k):
        return (
            tile.at[1], srow.at[mine], ss_r.at[k], rs_r.at[mine],
            y * NZ + z, jnp.int32(k), jnp.logical_and(on_diag, col == k),
        )

    def f_args(k):
        return (fsrc, frcv.at[col], ss_f.at[k], rs_f.at[col], row, jnp.int32(k), col == k)

    def reduce_tiles(p):
        for e in range(8):
            send(*a2a_args(p, e))

    def reduced(p):
        for k in range(8):
            arrived(a2a_rcv.at[p, k], rs_a.at[p, k])
        value = a2a_rcv[p, 0]
        for k in range(1, 8):
            value = value + a2a_rcv[p, k]
        return value

    def spread_z(p):
        for k in range(NZ):
            send(*z_args(p, k))

    def spread_x(p):
        for d in reversed(FAR):
            origin = (z + d) % NZ
            s = origin % 8

            @pl.when(origin // 8 == core)
            def _():
                for c in range(NC):
                    arrived(full.at[p, x, s, c], rs_z.at[p, s, c])
                for k in (2, 1, 3):
                    x_copy(p, k, s).start()

    def spread_done(p):
        for k in (1, 3, 2):
            other = (x + k) % NX
            for s in range(8):
                arrived(full.at[p, other, s], rs_x.at[p, other, s])
        parts = [full[p, :, s].reshape(NEW, 128) for s in range(8)]
        return jnp.concatenate(parts, axis=1)

    reduce_tiles(0)
    send(*e_args())
    for k in range(8):
        send(*g_args(k))

    tile[0] = matern(reduced(0)) * (1.0 / (18.0 * NOBS))
    spread_z(0)

    arrived(etr, rs_e)

    @pl.when(home)
    def _():
        for k in range(NZ):
            send(*ez_args(k))

    for k in range(8):
        arrived(grcv.at[k], rs_g.at[k])
    gram = grcv[0]
    for k in range(1, 8):
        gram = gram + grcv[k]
    gram = matern(gram[:, 0:NEW]) * (1.0 / NEW)
    gram = jnp.concatenate([gram, gram], axis=1)
    gram = jnp.where(lax.broadcasted_iota(jnp.int32, (8, 128), 1) // NEW == col // 4, gram, 0.0)
    cand_embed = jnp.broadcast_to(cand_embed_ref[...], (8, cand_ref.shape[0]))
    new_embed = jnp.dot(cand_embed, onehot, precision=HIGH, preferred_element_type=jnp.float32)[0:1]

    spread_x(0)
    kernel_cols = spread_done(0)
    inv_copy.wait()
    a2a_src[1] = dot_t(kernel_cols, inv[...], HIGH)
    reduce_tiles(1)
    tile[1] = reduced(1)
    spread_z(1)
    for k in range(8):
        send(*r_args(k))
    spread_x(1)
    solved_cols = spread_done(1)
    for s in range(8):
        arrived(ebuf.at[s], rs_ez.at[s])
    embed = jnp.concatenate([ebuf[s] for s in range(8)], axis=1)
    term = -dot_t(solved_cols, kernel_cols, HIGH)
    fsrc[0:HALF] = jnp.concatenate([term[0:HALF], term[HALF:]], axis=1)
    fsrc[HALF:HALF + 8, 0:NEW] = dot_t(jnp.broadcast_to(embed, (8, embed.shape[1])), solved_cols, HIGH)
    slot = pl.ds(pl.multiple_of(8 * (col % 4), 8), 8)
    fsrc[slot, :] = fsrc[slot, :] + gram
    for k in range(8):
        send(*f_args(k))
    solved_cols_ref[...] = solved_cols
    for k in range(8):
        arrived(srow.at[k], rs_r.at[k])
    solved_rows_ref[...] = srow[...].reshape(NEW, 128)
    for k in range(8):
        arrived(frcv.at[k], rs_f.at[k])
    total = frcv[0]
    for k in range(1, 8):
        total = total + frcv[k]
    total_ref[0:HALF] = total[0:HALF]
    total_ref[HALF:, 0:NEW] = total[HALF:, 0:NEW] * (1.0 / NOBS) - new_embed
    total_ref[HALF:, NEW:] = jnp.zeros((8, NEW), jnp.float32)

    wait_sent(*e_args())
    for p in range(2):
        for k in range(8):
            wait_sent(*a2a_args(p, k))
        for k in range(NZ):
            wait_sent(*z_args(p, k))
        for k in (1, 2, 3):
            for s in range(8):
                x_copy(p, k, s).wait_send()
    for k in range(8):
        wait_sent(*g_args(k))
        wait_sent(*r_args(k))
        wait_sent(*f_args(k))

    @pl.when(home)
    def _():
        for k in range(NZ):
            wait_sent(*ez_args(k))


def finish_kernel(
    total_ref, solved_cols_ref, solved_rows_ref, update_ref, inverse_ref, weights_ref, shift_ref,
):
    total = total_ref[...]
    sub = lax.broadcasted_iota(jnp.int32, (NEW, NEW), 0)
    lane = lax.broadcasted_iota(jnp.int32, (NEW, NEW), 1)
    eye = sub == lane
    matrix = jnp.concatenate([total[0:HALF, 0:NEW], total[0:HALF, NEW:]], axis=0) + jnp.where(eye, 1.0, 0.0)
    quad = jnp.sum(jnp.where(eye, total[HALF:HALF + 1, 0:NEW], 0.0), axis=1, keepdims=True)
    for base in range(0, NEW, GROUP):
        columns = [jnp.broadcast_to(matrix[:, k:k + 1], (NEW, NEW)) for k in range(base, base + GROUP)]
        for t in range(GROUP):
            k = base + t
            here = columns[t]
            pivot = here[k:k + 1, :]
            scale = jnp.where(pivot > 0.0, 1.0 / pivot, jnp.nan)
            at_lane, at_sub = lane == k, sub == k
            pivot_row = jnp.where(at_lane[0:1], 1.0, matrix[k:k + 1, :]) * scale
            matrix = jnp.where(at_sub, pivot_row, jnp.where(at_lane, 0.0, matrix) - here * pivot_row)
            for u in range(t + 1, GROUP):
                factor = columns[u][k:k + 1, :] * scale
                columns[u] = jnp.where(at_sub, factor, columns[u] - here * factor)
    inverse_ref[...] = matrix
    weights = jnp.sum(matrix * quad, axis=0, keepdims=True)
    weights_ref[...] = weights
    solved_rows = solved_rows_ref[...]
    shift_ref[...] = jnp.dot(
        jnp.broadcast_to(weights, (8, NEW)), solved_rows, precision=HIGH, preferred_element_type=jnp.float32
    )[0:1]
    left = jnp.dot(matrix, solved_rows, precision=HIGH, preferred_element_type=jnp.float32)
    update_ref[...] = lax.dot_general(
        left, solved_cols_ref[...], (((0,), (0,)), ((), ())), precision=HIGH, preferred_element_type=jnp.float32
    )


def on_device(inverse_kernel, points, candidates, obs_embed, cand_embed, chosen):
    rows, cols = inverse_kernel.shape
    f32 = jnp.float32
    vmem = pl.BlockSpec(memory_space=pltpu.VMEM)
    dma = pltpu.SemaphoreType.DMA
    total, solved_cols, solved_rows = pl.pallas_call(
        exchange_kernel,
        out_shape=(
            jax.ShapeDtypeStruct((HALF + 8, 128), f32),
            jax.ShapeDtypeStruct((NEW, cols), f32),
            jax.ShapeDtypeStruct((NEW, rows), f32),
        ),
        in_specs=[pl.BlockSpec(memory_space=pl.ANY)] + [vmem] * 5,
        out_specs=(vmem, vmem, vmem),
        scratch_shapes=[
            pltpu.VMEM((rows, cols), f32),
            pltpu.VMEM((2, NEW, 128), f32),
            pltpu.VMEM((2, 8, 8, 128), f32),
            pltpu.VMEM((2, 8, 128), f32),
            pltpu.VMEM((2, NX, 8, NC, 8, 128), f32),
            pltpu.VMEM((NEW, 128), f32),
            pltpu.VMEM((8, 8, 128), f32),
            pltpu.VMEM((1, 128), f32),
            pltpu.VMEM((8, 1, 128), f32),
            pltpu.VMEM((8, 8, 128), f32),
            pltpu.VMEM((HALF + 8, 128), f32),
            pltpu.VMEM((8, HALF + 8, 128), f32),
            dma((2, 8)), dma((2, 8)),
            dma((2, NZ)), dma((2, 8, NC)),
            dma((2, NX, 8)), dma((2, NX, 8)),
            dma((8,)), dma((8,)),
            dma((8,)), dma((8,)),
            dma((8,)), dma((8,)),
            dma, dma,
            dma((NZ,)), dma((8,)),
            dma,
        ],
        compiler_params=pltpu.CompilerParams(collective_id=0, has_side_effects=True),
    )(inverse_kernel, points, candidates, obs_embed.reshape(1, rows),
      chosen.reshape(1, NEW), cand_embed.reshape(1, -1))
    update, inverse, weights, shift = pl.pallas_call(
        finish_kernel,
        out_shape=(
            jax.ShapeDtypeStruct((rows, cols), f32),
            jax.ShapeDtypeStruct((NEW, NEW), f32),
            jax.ShapeDtypeStruct((1, NEW), f32),
            jax.ShapeDtypeStruct((1, rows), f32),
        ),
        in_specs=[vmem] * 3,
        out_specs=(vmem,) * 4,
    )(total, solved_cols, solved_rows)
    return update, inverse, weights.reshape(NEW), shift.reshape(rows)


def solution(mesh):
    return jax.shard_map(
        on_device,
        mesh=mesh,
        in_specs=(P("row", "col"), P("row", "col"), P(None, "col"), P("row"), P(), P()),
        out_specs=(P("row", "col"), P(), P(), P("row")),
        check_vma=False,
    )
```

```python
import jax
import jax.numpy as jnp
from jax import lax
from jax.experimental import pallas as pl
from jax.experimental.pallas import tpu as pltpu
from jax.sharding import PartitionSpec as P

MESH = pl.DeviceIdType.MESH
HIGH = lax.Precision.HIGHEST
NX, NY, NZ, NC = 4, 4, 16, 2
NOBS = 8192
NEW = 64
FAR = (8, 7, -7, 6, -6, 5, -5, 4, -4, 3, -3, 2, -2, 1, -1, 0)
GROUP = 4


def matern(square):
    scaled = jnp.sqrt(5.0 * jnp.maximum(square, 0.0))
    return (1.0 + scaled + scaled * scaled / 3.0) * jnp.exp(-scaled)


def dot_t(a, b, precision=None):
    return lax.dot_general(
        a, b, (((1,), (1,)), ((), ())), precision=precision, preferred_element_type=jnp.float32
    )


def exchange_kernel(
    inv_hbm, points_ref, cand_ref, embed_ref, chosen_ref, cand_embed_ref,
    total_ref, solved_cols_ref, solved_rows_ref,
    inv, inv_hi, inv_lo, a2a_src, a2a_rcv, tile, full, gsrc, grcv, gram, etr, ebuf, srow, fsrc, frcv, tot,
    ss_a, rs_a, ss_z, rs_z, ss_x, rs_x, ss_g, rs_g, ss_r, rs_r, ss_f, rs_f, ss_t, rs_t, ss_e, rs_e, ss_ez, rs_ez, inv_sem,
):
    row = lax.axis_index("row")
    col = lax.axis_index("col")
    x, z = row // NZ, row % NZ
    y, core = col // NC, col % NC
    half = z // 8
    spot = z % 8
    mine = 2 * x + core
    quarter = (x + 2) % NX
    own = (x, quarter)
    on_diag = x == y
    home = core == half

    def send(src, dst, ssem, rsem, to_row, to_col, is_self):
        remote = pltpu.make_async_remote_copy(
            src_ref=src, dst_ref=dst, send_sem=ssem, recv_sem=rsem,
            device_id=(to_row, to_col), device_id_type=MESH,
        )

        @pl.when(is_self)
        def _():
            pltpu.make_async_copy(src, dst, rsem).start()

        @pl.when(jnp.logical_not(is_self))
        def _():
            remote.start()

    def wait_sent(src, dst, ssem, rsem, to_row, to_col, is_self):
        @pl.when(jnp.logical_not(is_self))
        def _():
            pltpu.make_async_remote_copy(
                src_ref=src, dst_ref=dst, send_sem=ssem, recv_sem=rsem,
                device_id=(to_row, to_col), device_id_type=MESH,
            ).wait_send()

    def arrived(dst, rsem):
        pltpu.make_async_copy(dst, dst, rsem).wait()

    inv_copy = pltpu.make_async_copy(inv_hbm, inv, inv_sem)
    inv_copy.start()

    barrier = pltpu.get_barrier_semaphore()

    def greet(to_row, to_col, is_self):
        @pl.when(jnp.logical_not(is_self))
        def _():
            pl.semaphore_signal(barrier, inc=1, device_id=(to_row, to_col), device_id_type=MESH)

    for k in range(8):
        greet(y * NZ + z, jnp.int32(k), jnp.logical_and(on_diag, col == k))
        greet((k // 2) * NZ + z, x * NC + k % 2, jnp.logical_and(on_diag, mine == k))
        greet(row, jnp.int32(k), col == k)
    for k in range(16):
        greet(x * NZ + core * 8 + k // 2, y * NC + k % 2, jnp.logical_and(row % NZ == core * 8 + k // 2, core == k % 2))
    for k in range(4):
        greet(k * NZ + z, col, x == k)

    onehot = (chosen_ref[...] == lax.broadcasted_iota(jnp.int32, (cand_ref.shape[0], NEW), 0))
    onehot = jnp.where(onehot, 1.0, 0.0)
    appended = lax.dot_general(
        onehot.astype(jnp.bfloat16), cand_ref[...], (((0,), (0,)), ((), ())), preferred_element_type=jnp.float32
    ).astype(jnp.bfloat16)
    pts = points_ref[...]
    wide = pts.astype(jnp.float32)
    sq_obs = dot_t(jnp.ones((8, wide.shape[1]), jnp.float32), wide * wide, HIGH)[0:1]
    pair = dot_t(appended, appended)
    eye = lax.broadcasted_iota(jnp.int32, (NEW, NEW), 0) == lax.broadcasted_iota(jnp.int32, (NEW, NEW), 1)
    diagonal = jnp.where(eye, pair, 0.0)
    sq_col = jnp.sum(diagonal, axis=1, keepdims=True)
    sq_row = jnp.sum(diagonal, axis=0, keepdims=True)
    a2a_src[0] = sq_obs + sq_col - 2.0 * dot_t(appended, pts)
    gsrc[:, 0:NEW] = sq_row + sq_col - 2.0 * pair
    gsrc[:, NEW:] = jnp.zeros((NEW, NEW), jnp.float32)

    pl.semaphore_wait(barrier, 41 - 2 * on_diag.astype(jnp.int32) - home.astype(jnp.int32) + 1)

    never = x < 0

    def a2a_args(p, k, h):
        q = (x + k) % NX
        src = a2a_src.at[p, pl.ds(pl.multiple_of(16 * q + 8 * h, 8), 8)]
        is_self = jnp.logical_and(on_diag, core == h) if (k + 2 * p) % NX == 0 else never
        return (
            src, a2a_rcv.at[p, col], ss_a.at[p, k, h], rs_a.at[p, col],
            ((x + k + 2 * p) % NX) * NZ + z, x * NC + h, is_self,
        )

    def g_args(k):
        src = gsrc.at[pl.ds(pl.multiple_of(16 * quarter + 8 * k, 8), 8)]
        return (src, grcv.at[col], ss_g.at[k], rs_g.at[col], row, jnp.int32(k), col == k)

    def z_args(p, k):
        return (
            tile.at[p], full.at[p, own[p], spot, core], ss_z.at[p, k], rs_z.at[p, spot, core],
            x * NZ + (z + FAR[k]) % NZ, y * NC + half, jnp.logical_and(home, FAR[k] == 0),
        )

    def x_copy(p, k, s):
        return pltpu.make_async_remote_copy(
            src_ref=full.at[p, own[p], s], dst_ref=full.at[p, own[p], s],
            send_sem=ss_x.at[p, k, s], recv_sem=rs_x.at[p, own[p], s],
            device_id=(((x + k) % NX) * NZ + z, col), device_id_type=MESH,
        )

    def e_args():
        return (embed_ref, etr, ss_e, rs_e, y * NZ + z, x * NC + core, on_diag)

    def ez_args(k):
        return (etr, ebuf.at[spot], ss_ez.at[k], rs_ez.at[spot], x * NZ + k, y * NC + half, z == k)

    def r_args(k):
        return (
            tile.at[1], srow.at[2 * quarter + core], ss_r.at[k], rs_r.at[2 * quarter + core],
            y * NZ + z, jnp.int32(k), jnp.logical_and(on_diag, col == k),
        )

    def f_args(k):
        return (fsrc, frcv.at[col], ss_f.at[k], rs_f.at[col], row, (col + k) % 8, never if k else col >= 0)

    def t_copy(k):
        return pltpu.make_async_remote_copy(
            src_ref=tot.at[quarter], dst_ref=tot.at[quarter], send_sem=ss_t.at[k], recv_sem=rs_t.at[quarter],
            device_id=(((x + k) % NX) * NZ + z, col), device_id_type=MESH,
        )

    def reduced(p):
        for k in range(8):
            arrived(a2a_rcv.at[p, k], rs_a.at[p, k])
        value = a2a_rcv[p, 0]
        for k in range(1, 8):
            value = value + a2a_rcv[p, k]
        return value

    def spread_z(p):
        for k in range(NZ):
            send(*z_args(p, k))

    def spread_x(p):
        for d in reversed(FAR):
            origin = (z + d) % NZ
            s = origin % 8

            @pl.when(origin // 8 == core)
            def _():
                for c in range(NC):
                    arrived(full.at[p, own[p], s, c], rs_z.at[p, s, c])
                for k in (2, 1, 3):
                    x_copy(p, k, s).start()

    def x_arrived(p, k):
        other = (own[p] + k) % NX
        for s in range(8):
            arrived(full.at[p, other, s], rs_x.at[p, other, s])

    def block(p, q):
        return jnp.concatenate([full[p, q, s].reshape(16, 128) for s in range(8)], axis=1)

    def columns(p):
        return jnp.concatenate([full[p, :, s].reshape(NEW, 128) for s in range(8)], axis=1)

    for k in (2, 1, 3, 0):
        for h in range(NC):
            send(*a2a_args(0, k, h))
    send(*e_args())
    for k in range(2):
        send(*g_args(k))

    tile[0] = matern(reduced(0)) * (1.0 / (18.0 * NOBS))
    spread_z(0)

    arrived(etr, rs_e)

    @pl.when(home)
    def _():
        for k in range(NZ):
            send(*ez_args(k))

    gram[...] = jnp.zeros((16, 128), jnp.float32)

    @pl.when(col < 2)
    def _():
        for k in range(8):
            arrived(grcv.at[k], rs_g.at[k])
        value = grcv[0]
        for k in range(1, 8):
            value = value + grcv[k]
        gram[pl.ds(pl.multiple_of(8 * (col % 2), 8), 8), 0:NEW] = matern(value[:, 0:NEW]) * (1.0 / NEW)

    cand_embed = jnp.broadcast_to(cand_embed_ref[...], (8, cand_ref.shape[0]))
    new_embed = jnp.dot(cand_embed, onehot, precision=HIGH, preferred_element_type=jnp.float32)[0:1]
    new_embed = jnp.sum(jnp.where(eye, new_embed, 0.0), axis=1, keepdims=True)
    inv_copy.wait()
    whole = inv[...]
    inv_hi[...] = whole.astype(jnp.bfloat16)
    inv_lo[...] = (whole - whole.astype(jnp.bfloat16).astype(jnp.float32)).astype(jnp.bfloat16)

    spread_x(0)
    for k in (0, 1, 3, 2):
        if k:
            x_arrived(0, k)
        q = (x + k) % NX
        value = block(0, q)
        hi = value.astype(jnp.bfloat16)
        lo = (value - hi.astype(jnp.float32)).astype(jnp.bfloat16)
        both = dot_t(jnp.concatenate([hi, lo], axis=0), inv_hi[...])
        a2a_src[1, pl.ds(pl.multiple_of(16 * q, 8), 16)] = both[0:16] + both[16:32] + dot_t(hi, inv_lo[...])
        for h in range(NC):
            send(*a2a_args(1, k, h))
    kernel_cols = columns(0)
    for s in range(8):
        arrived(ebuf.at[s], rs_ez.at[s])
    embed = jnp.concatenate([ebuf[s] for s in range(8)], axis=1)
    tile[1] = reduced(1)
    spread_z(1)
    for k in range(8):
        send(*r_args(k))
    spread_x(1)
    solved = block(1, quarter)
    fsrc[:, 0:NEW] = gram[:, 0:NEW] - dot_t(solved, kernel_cols, HIGH)
    fsrc[:, NEW:] = jnp.broadcast_to(jnp.sum(solved * embed, axis=1, keepdims=True), (16, NEW))
    for k in (4, 3, 5, 2, 6, 1, 7, 0):
        send(*f_args(k))
    for k in range(8):
        arrived(srow.at[k], rs_r.at[k])
    solved_rows_ref[...] = srow[...].reshape(NEW, 128)
    for k in range(8):
        arrived(frcv.at[k], rs_f.at[k])
    total = frcv[0]
    for k in range(1, 8):
        total = total + frcv[k]
    tot[quarter] = total
    for k in (2, 1, 3):
        t_copy(k).start()
    for k in (1, 3, 2):
        x_arrived(1, k)
    solved_cols_ref[...] = columns(1)
    for k in (1, 3, 2):
        other = (quarter + k) % NX
        arrived(tot.at[other], rs_t.at[other])
    total = tot[...].reshape(NEW, 128)
    total_ref[:, 0:NEW] = total[:, 0:NEW]
    total_ref[:, NEW:] = total[:, NEW:] * (1.0 / NOBS) - new_embed

    wait_sent(*e_args())
    for p in range(2):
        for k in range(NX):
            for h in range(NC):
                wait_sent(*a2a_args(p, k, h))
        for k in range(NZ):
            wait_sent(*z_args(p, k))
        for k in (1, 2, 3):
            for s in range(8):
                x_copy(p, k, s).wait_send()
    for k in (1, 2, 3):
        t_copy(k).wait_send()
    for k in range(2):
        wait_sent(*g_args(k))
    for k in range(8):
        wait_sent(*r_args(k))
        wait_sent(*f_args(k))

    @pl.when(home)
    def _():
        for k in range(NZ):
            wait_sent(*ez_args(k))


def finish_kernel(
    total_ref, solved_cols_ref, solved_rows_ref, update_ref, inverse_ref, weights_ref, shift_ref,
):
    total = total_ref[...]
    sub = lax.broadcasted_iota(jnp.int32, (NEW, NEW), 0)
    lane = lax.broadcasted_iota(jnp.int32, (NEW, NEW), 1)
    eye = sub == lane
    matrix = total[:, 0:NEW] + jnp.where(eye, 1.0, 0.0)
    quad = total[:, NEW:NEW + 1]
    for base in range(0, NEW, GROUP):
        columns = [jnp.broadcast_to(matrix[:, k:k + 1], (NEW, NEW)) for k in range(base, base + GROUP)]
        for t in range(GROUP):
            k = base + t
            here = columns[t]
            pivot = here[k:k + 1, :]
            scale = jnp.where(pivot > 0.0, 1.0 / pivot, jnp.nan)
            at_lane, at_sub = lane == k, sub == k
            pivot_row = jnp.where(at_lane[0:1], 1.0, matrix[k:k + 1, :]) * scale
            matrix = jnp.where(at_sub, pivot_row, jnp.where(at_lane, 0.0, matrix) - here * pivot_row)
            for u in range(t + 1, GROUP):
                factor = columns[u][k:k + 1, :] * scale
                columns[u] = jnp.where(at_sub, factor, columns[u] - here * factor)
    inverse_ref[...] = matrix
    weights = jnp.sum(matrix * quad, axis=0, keepdims=True)
    weights_ref[...] = weights
    solved_rows = solved_rows_ref[...]
    shift_ref[...] = jnp.dot(
        jnp.broadcast_to(weights, (8, NEW)), solved_rows, precision=HIGH, preferred_element_type=jnp.float32
    )[0:1]
    left = jnp.dot(matrix, solved_rows, precision=HIGH, preferred_element_type=jnp.float32)
    update_ref[...] = lax.dot_general(
        left, solved_cols_ref[...], (((0,), (0,)), ((), ())), precision=HIGH, preferred_element_type=jnp.float32
    )


def on_device(inverse_kernel, points, candidates, obs_embed, cand_embed, chosen):
    rows, cols = inverse_kernel.shape
    f32 = jnp.float32
    vmem = pl.BlockSpec(memory_space=pltpu.VMEM)
    dma = pltpu.SemaphoreType.DMA
    total, solved_cols, solved_rows = pl.pallas_call(
        exchange_kernel,
        out_shape=(
            jax.ShapeDtypeStruct((NEW, 128), f32),
            jax.ShapeDtypeStruct((NEW, cols), f32),
            jax.ShapeDtypeStruct((NEW, rows), f32),
        ),
        in_specs=[pl.BlockSpec(memory_space=pl.ANY)] + [vmem] * 5,
        out_specs=(vmem, vmem, vmem),
        scratch_shapes=[
            pltpu.VMEM((rows, cols), f32),
            pltpu.VMEM((rows, cols), jnp.bfloat16),
            pltpu.VMEM((rows, cols), jnp.bfloat16),
            pltpu.VMEM((2, NEW, 128), f32),
            pltpu.VMEM((2, 8, 8, 128), f32),
            pltpu.VMEM((2, 8, 128), f32),
            pltpu.VMEM((2, NX, 8, NC, 8, 128), f32),
            pltpu.VMEM((NEW, 128), f32),
            pltpu.VMEM((8, 8, 128), f32),
            pltpu.VMEM((16, 128), f32),
            pltpu.VMEM((1, 128), f32),
            pltpu.VMEM((8, 1, 128), f32),
            pltpu.VMEM((8, 8, 128), f32),
            pltpu.VMEM((16, 128), f32),
            pltpu.VMEM((8, 16, 128), f32),
            pltpu.VMEM((NX, 16, 128), f32),
            dma((2, NX, NC)), dma((2, 8)),
            dma((2, NZ)), dma((2, 8, NC)),
            dma((2, NX, 8)), dma((2, NX, 8)),
            dma((2,)), dma((8,)),
            dma((8,)), dma((8,)),
            dma((8,)), dma((8,)),
            dma((NX,)), dma((NX,)),
            dma, dma,
            dma((NZ,)), dma((8,)),
            dma,
        ],
        compiler_params=pltpu.CompilerParams(collective_id=0, has_side_effects=True),
    )(inverse_kernel, points, candidates, obs_embed.reshape(1, rows),
      chosen.reshape(1, NEW), cand_embed.reshape(1, -1))
    update, inverse, weights, shift = pl.pallas_call(
        finish_kernel,
        out_shape=(
            jax.ShapeDtypeStruct((rows, cols), f32),
            jax.ShapeDtypeStruct((NEW, NEW), f32),
            jax.ShapeDtypeStruct((1, NEW), f32),
            jax.ShapeDtypeStruct((1, rows), f32),
        ),
        in_specs=[vmem] * 3,
        out_specs=(vmem,) * 4,
    )(total, solved_cols, solved_rows)
    return update, inverse, weights.reshape(NEW), shift.reshape(rows)


def solution(mesh):
    return jax.shard_map(
        on_device,
        mesh=mesh,
        in_specs=(P("row", "col"), P("row", "col"), P(None, "col"), P("row"), P(), P()),
        out_specs=(P("row", "col"), P(), P(), P("row")),
        check_vma=False,
    )
```

```python
import jax
import jax.numpy as jnp
from jax import lax
from jax.experimental import pallas as pl
from jax.experimental.pallas import tpu as pltpu
from jax.sharding import PartitionSpec as P

MESH = pl.DeviceIdType.MESH
HIGH = lax.Precision.HIGHEST
NX, NY, NZ, NC = 4, 4, 16, 2
NOBS = 8192
NEW = 64
FAR = (8, 7, -7, 6, -6, 5, -5, 4, -4, 3, -3, 2, -2, 1, -1, 0)
GROUP = 4


def matern(square):
    scaled = jnp.sqrt(5.0 * jnp.maximum(square, 0.0))
    return (1.0 + scaled + scaled * scaled / 3.0) * jnp.exp(-scaled)


def dot_t(a, b, precision=None):
    return lax.dot_general(
        a, b, (((1,), (1,)), ((), ())), precision=precision, preferred_element_type=jnp.float32
    )


def exchange_kernel(
    inv_hbm, points_ref, cand_ref, embed_ref, chosen_ref, cand_embed_ref,
    total_ref, solved_cols_ref, solved_rows_ref,
    inv, inv_hi, inv_lo, a2a_src, a2a_rcv, tile, full, gsrc, grcv, gram, etr, ebuf, srow, fsrc, frcv, tot,
    ss_a, rs_a, ss_z, rs_z, ss_x, rs_x, ss_g, rs_g, ss_r, rs_r, ss_f, rs_f, ss_t, rs_t, ss_e, rs_e, ss_ez, rs_ez, inv_sem, out_sem, scols, srows, ready,
):
    row = lax.axis_index("row")
    col = lax.axis_index("col")
    x, z = row // NZ, row % NZ
    y, core = col // NC, col % NC
    half = z // 8
    spot = z % 8
    mine = 2 * x + core
    quarter = (x + 2) % NX
    own = (x, quarter)
    on_diag = x == y
    home = core == half

    def send(src, dst, ssem, rsem, to_row, to_col, is_self):
        remote = pltpu.make_async_remote_copy(
            src_ref=src, dst_ref=dst, send_sem=ssem, recv_sem=rsem,
            device_id=(to_row, to_col), device_id_type=MESH,
        )

        @pl.when(is_self)
        def _():
            pltpu.make_async_copy(src, dst, rsem).start()

        @pl.when(jnp.logical_not(is_self))
        def _():
            remote.start()

    def wait_sent(src, dst, ssem, rsem, to_row, to_col, is_self):
        @pl.when(jnp.logical_not(is_self))
        def _():
            pltpu.make_async_remote_copy(
                src_ref=src, dst_ref=dst, send_sem=ssem, recv_sem=rsem,
                device_id=(to_row, to_col), device_id_type=MESH,
            ).wait_send()

    def arrived(dst, rsem):
        pltpu.make_async_copy(dst, dst, rsem).wait()

    inv_copy = pltpu.make_async_copy(inv_hbm, inv, inv_sem)
    inv_copy.start()

    barrier = pltpu.get_barrier_semaphore()

    def greet(to_row, to_col, is_self):
        @pl.when(jnp.logical_not(is_self))
        def _():
            pl.semaphore_signal(barrier, inc=1, device_id=(to_row, to_col), device_id_type=MESH)

    for k in range(8):
        greet(y * NZ + z, jnp.int32(k), jnp.logical_and(on_diag, col == k))
        greet((k // 2) * NZ + z, x * NC + k % 2, jnp.logical_and(on_diag, mine == k))
        greet(row, jnp.int32(k), col == k)
    for d in (4, -4, 3, -3, 2, -2, 1, -1):
        for h in range(NC):
            greet(x * NZ + (z + d) % NZ, y * NC + h, x < 0)
    for k in range(4):
        greet(k * NZ + z, col, x == k)

    onehot = (chosen_ref[...] == lax.broadcasted_iota(jnp.int32, (cand_ref.shape[0], NEW), 0))
    onehot = jnp.where(onehot, 1.0, 0.0)
    appended = lax.dot_general(
        onehot.astype(jnp.bfloat16), cand_ref[...], (((0,), (0,)), ((), ())), preferred_element_type=jnp.float32
    ).astype(jnp.bfloat16)
    pts = points_ref[...]
    wide = pts.astype(jnp.float32)
    sq_obs = dot_t(jnp.ones((8, wide.shape[1]), jnp.float32), wide * wide, HIGH)[0:1]
    eye = lax.broadcasted_iota(jnp.int32, (NEW, NEW), 0) == lax.broadcasted_iota(jnp.int32, (NEW, NEW), 1)
    new = appended.astype(jnp.float32)
    sq_col = jnp.sum(new * new, axis=1, keepdims=True)
    a2a_src[0] = sq_obs + sq_col - 2.0 * dot_t(appended, pts)

    pl.semaphore_wait(barrier, 42 - 2 * on_diag.astype(jnp.int32))
    for d in (4, -4):
        pl.semaphore_signal(ready, inc=1, device_id=(x * NZ + (z + d) % NZ, col), device_id_type=MESH)

    never = x < 0

    def a2a_args(p, k, h):
        q = (x + k) % NX
        src = a2a_src.at[p, pl.ds(pl.multiple_of(16 * q + 8 * h, 8), 8)]
        is_self = jnp.logical_and(on_diag, core == h) if (k + 2 * p) % NX == 0 else never
        return (
            src, a2a_rcv.at[p, col], ss_a.at[p, k, h], rs_a.at[p, col],
            ((x + k + 2 * p) % NX) * NZ + z, x * NC + h, is_self,
        )

    def g_args(k):
        src = gsrc.at[pl.ds(pl.multiple_of(16 * quarter + 8 * k, 8), 8)]
        return (src, grcv.at[col], ss_g.at[k], rs_g.at[col], row, jnp.int32(k), col == k)

    def z_args(p, k):
        return (
            tile.at[p], full.at[p, own[p], spot, core], ss_z.at[p, k], rs_z.at[p, spot, core],
            x * NZ + (z + FAR[k]) % NZ, y * NC + half, jnp.logical_and(home, FAR[k] == 0),
        )

    def x_copy(p, k, s):
        return pltpu.make_async_remote_copy(
            src_ref=full.at[p, own[p], s], dst_ref=full.at[p, own[p], s],
            send_sem=ss_x.at[p, k, s], recv_sem=rs_x.at[p, own[p], s],
            device_id=(((x + k) % NX) * NZ + z, col), device_id_type=MESH,
        )

    def e_args():
        return (embed_ref, etr, ss_e, rs_e, y * NZ + z, x * NC + core, on_diag)

    def ez_args(k):
        return (etr, ebuf.at[spot], ss_ez.at[k], rs_ez.at[spot], x * NZ + k, y * NC + half, z == k)

    def r_args(k):
        return (
            tile.at[1], srow.at[2 * quarter + core], ss_r.at[k], rs_r.at[2 * quarter + core],
            y * NZ + z, jnp.int32(k), jnp.logical_and(on_diag, col == k),
        )

    def f_args(k):
        return (fsrc, frcv.at[col], ss_f.at[k], rs_f.at[col], row, (col + k) % 8, never if k else col >= 0)

    def t_copy(k):
        return pltpu.make_async_remote_copy(
            src_ref=tot.at[quarter], dst_ref=tot.at[quarter], send_sem=ss_t.at[k], recv_sem=rs_t.at[quarter],
            device_id=(((x + k) % NX) * NZ + z, col), device_id_type=MESH,
        )

    def reduced(p):
        for k in range(8):
            arrived(a2a_rcv.at[p, k], rs_a.at[p, k])
        value = a2a_rcv[p, 0]
        for k in range(1, 8):
            value = value + a2a_rcv[p, k]
        return value

    def spread_z(p):
        for k in range(NZ):
            send(*z_args(p, k))

    def spread_x(p):
        for d in reversed(FAR):
            origin = (z + d) % NZ
            s = origin % 8

            @pl.when(origin // 8 == core)
            def _():
                for c in range(NC):
                    arrived(full.at[p, own[p], s, c], rs_z.at[p, s, c])
                for k in (2, 1, 3):
                    x_copy(p, k, s).start()

    def x_arrived(p, k):
        other = (own[p] + k) % NX
        for s in range(8):
            arrived(full.at[p, other, s], rs_x.at[p, other, s])

    def block(p, q):
        return jnp.concatenate([full[p, q, s].reshape(16, 128) for s in range(8)], axis=1)

    def columns(p):
        return jnp.concatenate([full[p, :, s].reshape(NEW, 128) for s in range(8)], axis=1)

    for k in (2, 1, 3, 0):
        for h in range(NC):
            send(*a2a_args(0, k, h))
    send(*e_args())

    pair = dot_t(appended, appended)
    diagonal = jnp.where(eye, pair, 0.0)
    sq_row = jnp.sum(diagonal, axis=0, keepdims=True)
    sq_col = jnp.sum(diagonal, axis=1, keepdims=True)
    gsrc[:, 0:NEW] = sq_row + sq_col - 2.0 * pair
    gsrc[:, NEW:] = jnp.zeros((NEW, NEW), jnp.float32)

    tile[0] = matern(reduced(0)) * (1.0 / (18.0 * NOBS))
    pl.semaphore_wait(ready, 2)
    spread_z(0)
    for k in range(2):
        send(*g_args(k))

    arrived(etr, rs_e)

    @pl.when(home)
    def _():
        for k in range(NZ):
            send(*ez_args(k))

    gram[...] = jnp.zeros((16, 128), jnp.float32)

    @pl.when(col < 2)
    def _():
        for k in range(8):
            arrived(grcv.at[k], rs_g.at[k])
        value = grcv[0]
        for k in range(1, 8):
            value = value + grcv[k]
        gram[pl.ds(pl.multiple_of(8 * (col % 2), 8), 8), 0:NEW] = matern(value[:, 0:NEW]) * (1.0 / NEW)

    cand_embed = jnp.broadcast_to(cand_embed_ref[...], (8, cand_ref.shape[0]))
    new_embed = jnp.dot(cand_embed, onehot, precision=HIGH, preferred_element_type=jnp.float32)[0:1]
    new_embed = jnp.sum(jnp.where(eye, new_embed, 0.0), axis=1, keepdims=True)
    inv_copy.wait()
    whole = inv[...]
    inv_hi[...] = whole.astype(jnp.bfloat16)
    inv_lo[...] = (whole - whole.astype(jnp.bfloat16).astype(jnp.float32)).astype(jnp.bfloat16)

    spread_x(0)
    for k in (0, 1, 3, 2):
        if k:
            x_arrived(0, k)
        q = (x + k) % NX
        value = block(0, q)
        hi = value.astype(jnp.bfloat16)
        lo = (value - hi.astype(jnp.float32)).astype(jnp.bfloat16)
        both = dot_t(jnp.concatenate([hi, lo], axis=0), inv_hi[...])
        a2a_src[1, pl.ds(pl.multiple_of(16 * q, 8), 16)] = both[0:16] + both[16:32] + dot_t(hi, inv_lo[...])
        for h in range(NC):
            send(*a2a_args(1, k, h))
    kernel_cols = columns(0)
    for s in range(8):
        arrived(ebuf.at[s], rs_ez.at[s])
    embed = jnp.concatenate([ebuf[s] for s in range(8)], axis=1)
    tile[1] = reduced(1)
    spread_z(1)
    for k in range(8):
        send(*r_args(k))
    spread_x(1)
    solved = block(1, quarter)
    fsrc[:, 0:NEW] = gram[:, 0:NEW] - dot_t(solved, kernel_cols, HIGH)
    fsrc[:, NEW:] = jnp.broadcast_to(jnp.sum(solved * embed, axis=1, keepdims=True), (16, NEW))
    for k in (4, 3, 5, 2, 6, 1, 7, 0):
        send(*f_args(k))
    for k in range(8):
        arrived(srow.at[k], rs_r.at[k])
    srows[...] = srow[...].reshape(NEW, 128)
    rows_out = pltpu.make_async_copy(srows, solved_rows_ref, out_sem.at[0])
    rows_out.start()
    for k in range(8):
        arrived(frcv.at[k], rs_f.at[k])
    total = frcv[0]
    for k in range(1, 8):
        total = total + frcv[k]
    tot[quarter] = total
    for k in (2, 1, 3):
        t_copy(k).start()
    for k in (1, 3, 2):
        x_arrived(1, k)
    scols[...] = columns(1)
    cols_out = pltpu.make_async_copy(scols, solved_cols_ref, out_sem.at[1])
    cols_out.start()
    for k in (1, 3, 2):
        other = (quarter + k) % NX
        arrived(tot.at[other], rs_t.at[other])
    total = tot[...].reshape(NEW, 128)
    total_ref[:, 0:NEW] = total[:, 0:NEW]
    total_ref[:, NEW:] = total[:, NEW:] * (1.0 / NOBS) - new_embed

    rows_out.wait()
    cols_out.wait()
    wait_sent(*e_args())
    for p in range(2):
        for k in range(NX):
            for h in range(NC):
                wait_sent(*a2a_args(p, k, h))
        for k in range(NZ):
            wait_sent(*z_args(p, k))
        for k in (1, 2, 3):
            for s in range(8):
                x_copy(p, k, s).wait_send()
    for k in (1, 2, 3):
        t_copy(k).wait_send()
    for k in range(2):
        wait_sent(*g_args(k))
    for k in range(8):
        wait_sent(*r_args(k))
        wait_sent(*f_args(k))

    @pl.when(home)
    def _():
        for k in range(NZ):
            wait_sent(*ez_args(k))


def finish_kernel(
    total_ref, solved_cols_ref, solved_rows_ref, update_ref, inverse_ref, weights_ref, shift_ref,
):
    total = total_ref[...]
    sub = lax.broadcasted_iota(jnp.int32, (NEW, NEW), 0)
    lane = lax.broadcasted_iota(jnp.int32, (NEW, NEW), 1)
    eye = sub == lane
    matrix = total[:, 0:NEW] + jnp.where(eye, 1.0, 0.0)
    quad = total[:, NEW:NEW + 1]
    for base in range(0, NEW, GROUP):
        columns = [jnp.broadcast_to(matrix[:, k:k + 1], (NEW, NEW)) for k in range(base, base + GROUP)]
        for t in range(GROUP):
            k = base + t
            here = columns[t]
            pivot = here[k:k + 1, :]
            scale = jnp.where(pivot > 0.0, 1.0 / pivot, jnp.nan)
            at_lane, at_sub = lane == k, sub == k
            pivot_row = jnp.where(at_lane[0:1], 1.0, matrix[k:k + 1, :]) * scale
            matrix = jnp.where(at_sub, pivot_row, jnp.where(at_lane, 0.0, matrix) - here * pivot_row)
            for u in range(t + 1, GROUP):
                factor = columns[u][k:k + 1, :] * scale
                columns[u] = jnp.where(at_sub, factor, columns[u] - here * factor)
    inverse_ref[...] = matrix
    weights = jnp.sum(matrix * quad, axis=0, keepdims=True)
    weights_ref[...] = weights
    solved_rows = solved_rows_ref[...]
    shift_ref[...] = jnp.dot(
        jnp.broadcast_to(weights, (8, NEW)), solved_rows, precision=HIGH, preferred_element_type=jnp.float32
    )[0:1]
    left = jnp.dot(matrix, solved_rows, precision=HIGH, preferred_element_type=jnp.float32)
    update_ref[...] = lax.dot_general(
        left, solved_cols_ref[...], (((0,), (0,)), ((), ())), precision=HIGH, preferred_element_type=jnp.float32
    )


def on_device(inverse_kernel, points, candidates, obs_embed, cand_embed, chosen):
    rows, cols = inverse_kernel.shape
    f32 = jnp.float32
    vmem = pl.BlockSpec(memory_space=pltpu.VMEM)
    dma = pltpu.SemaphoreType.DMA
    total, solved_cols, solved_rows = pl.pallas_call(
        exchange_kernel,
        out_shape=(
            jax.ShapeDtypeStruct((NEW, 128), f32),
            jax.ShapeDtypeStruct((NEW, cols), f32),
            jax.ShapeDtypeStruct((NEW, rows), f32),
        ),
        in_specs=[pl.BlockSpec(memory_space=pl.ANY)] + [vmem] * 5,
        out_specs=(vmem, pl.BlockSpec(memory_space=pl.ANY), pl.BlockSpec(memory_space=pl.ANY)),
        scratch_shapes=[
            pltpu.VMEM((rows, cols), f32),
            pltpu.VMEM((rows, cols), jnp.bfloat16),
            pltpu.VMEM((rows, cols), jnp.bfloat16),
            pltpu.VMEM((2, NEW, 128), f32),
            pltpu.VMEM((2, 8, 8, 128), f32),
            pltpu.VMEM((2, 8, 128), f32),
            pltpu.VMEM((2, NX, 8, NC, 8, 128), f32),
            pltpu.VMEM((NEW, 128), f32),
            pltpu.VMEM((8, 8, 128), f32),
            pltpu.VMEM((16, 128), f32),
            pltpu.VMEM((1, 128), f32),
            pltpu.VMEM((8, 1, 128), f32),
            pltpu.VMEM((8, 8, 128), f32),
            pltpu.VMEM((16, 128), f32),
            pltpu.VMEM((8, 16, 128), f32),
            pltpu.VMEM((NX, 16, 128), f32),
            dma((2, NX, NC)), dma((2, 8)),
            dma((2, NZ)), dma((2, 8, NC)),
            dma((2, NX, 8)), dma((2, NX, 8)),
            dma((2,)), dma((8,)),
            dma((8,)), dma((8,)),
            dma((8,)), dma((8,)),
            dma((NX,)), dma((NX,)),
            dma, dma,
            dma((NZ,)), dma((8,)),
            dma,
            dma((2,)),
            pltpu.VMEM((NEW, cols), f32),
            pltpu.VMEM((NEW, rows), f32),
            pltpu.SemaphoreType.REGULAR,
        ],
        compiler_params=pltpu.CompilerParams(collective_id=0, has_side_effects=True),
    )(inverse_kernel, points, candidates, obs_embed.reshape(1, rows),
      chosen.reshape(1, NEW), cand_embed.reshape(1, -1))
    update, inverse, weights, shift = pl.pallas_call(
        finish_kernel,
        out_shape=(
            jax.ShapeDtypeStruct((rows, cols), f32),
            jax.ShapeDtypeStruct((NEW, NEW), f32),
            jax.ShapeDtypeStruct((1, NEW), f32),
            jax.ShapeDtypeStruct((1, rows), f32),
        ),
        in_specs=[vmem] * 3,
        out_specs=(vmem,) * 4,
    )(total, solved_cols, solved_rows)
    return update, inverse, weights.reshape(NEW), shift.reshape(rows)


def solution(mesh):
    return jax.shard_map(
        on_device,
        mesh=mesh,
        in_specs=(P("row", "col"), P("row", "col"), P(None, "col"), P("row"), P(), P()),
        out_specs=(P("row", "col"), P(), P(), P("row")),
        check_vma=False,
    )
```

```python
import jax
import jax.numpy as jnp
from jax import lax
from jax.experimental import pallas as pl
from jax.experimental.pallas import tpu as pltpu
from jax.sharding import PartitionSpec as P

MESH = pl.DeviceIdType.MESH
HIGH = lax.Precision.HIGHEST
NX, NY, NZ, NC = 4, 4, 16, 2
NOBS = 8192
NEW = 64
FAR = (8, 7, -7, 6, -6, 5, -5, 4, -4, 3, -3, 2, -2, 1, -1, 0)
GROUP = 8


def matern(square):
    scaled = jnp.sqrt(5.0 * jnp.maximum(square, 0.0))
    return (1.0 + scaled + scaled * scaled / 3.0) * jnp.exp(-scaled)


def dot_t(a, b, precision=None):
    return lax.dot_general(
        a, b, (((1,), (1,)), ((), ())), precision=precision, preferred_element_type=jnp.float32
    )


def split(value):
    hi = value.astype(jnp.bfloat16)
    return hi, (value - hi.astype(jnp.float32)).astype(jnp.bfloat16)


def exchange_kernel(
    inv_hbm, points_hbm, cand_hbm, embed_hbm, chosen_hbm, cand_embed_hbm,
    total_ref, solved_cols_ref, solved_rows_ref,
    inv, inv_hi, inv_lo, a2a_src, a2a_rcv, tile, full, gsrc, grcv, gram, etr, ebuf, srow, fsrc, frcv, tot,
    ss_a, rs_a, ss_z, rs_z, ss_x, rs_x, ss_g, rs_g, ss_r, rs_r, ss_f, rs_f, ss_t, rs_t, ss_e, rs_e, ss_ez, rs_ez, inv_sem, out_sem, scols, srows, ready,
    points_ref, cand_ref, embed_ref, chosen_ref, cand_embed_ref, in_sem,
):
    row = lax.axis_index("row")
    col = lax.axis_index("col")
    x, z = row // NZ, row % NZ
    y, core = col // NC, col % NC
    half = z // 8
    spot = z % 8
    mine = 2 * x + core
    quarter = (x + 2) % NX
    own = (x, quarter)
    on_diag = x == y
    home = core == half

    def send(src, dst, ssem, rsem, to_row, to_col, is_self):
        remote = pltpu.make_async_remote_copy(
            src_ref=src, dst_ref=dst, send_sem=ssem, recv_sem=rsem,
            device_id=(to_row, to_col), device_id_type=MESH,
        )

        @pl.when(is_self)
        def _():
            pltpu.make_async_copy(src, dst, rsem).start()

        @pl.when(jnp.logical_not(is_self))
        def _():
            remote.start()

    def wait_sent(src, dst, ssem, rsem, to_row, to_col, is_self):
        @pl.when(jnp.logical_not(is_self))
        def _():
            pltpu.make_async_remote_copy(
                src_ref=src, dst_ref=dst, send_sem=ssem, recv_sem=rsem,
                device_id=(to_row, to_col), device_id_type=MESH,
            ).wait_send()

    def arrived(dst, rsem):
        pltpu.make_async_copy(dst, dst, rsem).wait()

    loads = [
        pltpu.make_async_copy(src, dst, in_sem.at[k])
        for k, (src, dst) in enumerate((
            (chosen_hbm, chosen_ref), (cand_hbm, cand_ref), (points_hbm, points_ref),
            (embed_hbm, embed_ref), (cand_embed_hbm, cand_embed_ref),
        ))
    ]
    for load in loads:
        load.start()
    inv_copy = pltpu.make_async_copy(inv_hbm, inv, inv_sem)
    inv_copy.start()

    barrier = pltpu.get_barrier_semaphore()

    def greet(to_row, to_col, is_self):
        @pl.when(jnp.logical_not(is_self))
        def _():
            pl.semaphore_signal(barrier, inc=1, device_id=(to_row, to_col), device_id_type=MESH)

    for k in range(8):
        greet(y * NZ + z, jnp.int32(k), jnp.logical_and(on_diag, col == k))
        greet((k // 2) * NZ + z, x * NC + k % 2, jnp.logical_and(on_diag, mine == k))
        greet(row, jnp.int32(k), col == k)
    for d in (4, -4, 3, -3, 2, -2, 1, -1):
        for h in range(NC):
            greet(x * NZ + (z + d) % NZ, y * NC + h, x < 0)
    for k in range(4):
        greet(k * NZ + z, col, x == k)

    for load in loads:
        load.wait()
    onehot = (chosen_ref[...] == lax.broadcasted_iota(jnp.int32, (cand_ref.shape[0], NEW), 0))
    onehot = jnp.where(onehot, 1.0, 0.0)
    appended = lax.dot_general(
        onehot.astype(jnp.bfloat16), cand_ref[...], (((0,), (0,)), ((), ())), preferred_element_type=jnp.float32
    ).astype(jnp.bfloat16)
    pts = points_ref[...]
    wide = pts.astype(jnp.float32)
    ones = jnp.ones((8, wide.shape[1]), jnp.bfloat16)
    sq_hi, sq_lo = split(wide * wide)
    sq_obs = (dot_t(ones, sq_hi) + dot_t(ones, sq_lo))[0:1]
    eye = lax.broadcasted_iota(jnp.int32, (NEW, NEW), 0) == lax.broadcasted_iota(jnp.int32, (NEW, NEW), 1)
    new = appended.astype(jnp.float32)
    sq_col = jnp.sum(new * new, axis=1, keepdims=True)
    a2a_src[0] = sq_obs + sq_col - 2.0 * dot_t(appended, pts)

    pl.semaphore_wait(barrier, 42 - 2 * on_diag.astype(jnp.int32))
    for d in (4, -4):
        pl.semaphore_signal(ready, inc=1, device_id=(x * NZ + (z + d) % NZ, col), device_id_type=MESH)

    never = x < 0

    def a2a_args(p, k, h):
        q = (x + k) % NX
        src = a2a_src.at[p, pl.ds(pl.multiple_of(16 * q + 8 * h, 8), 8)]
        is_self = jnp.logical_and(on_diag, core == h) if (k + 2 * p) % NX == 0 else never
        return (
            src, a2a_rcv.at[p, col], ss_a.at[p, k, h], rs_a.at[p, col],
            ((x + k + 2 * p) % NX) * NZ + z, x * NC + h, is_self,
        )

    def g_args(k):
        src = gsrc.at[pl.ds(pl.multiple_of(16 * quarter + 8 * k, 8), 8)]
        return (src, grcv.at[col], ss_g.at[k], rs_g.at[col], row, jnp.int32(k), col == k)

    def z_args(p, k):
        return (
            tile.at[p], full.at[p, own[p], spot, core], ss_z.at[p, k], rs_z.at[p, spot, core],
            x * NZ + (z + FAR[k]) % NZ, y * NC + half, jnp.logical_and(home, FAR[k] == 0),
        )

    def x_copy(p, k, s):
        return pltpu.make_async_remote_copy(
            src_ref=full.at[p, own[p], s], dst_ref=full.at[p, own[p], s],
            send_sem=ss_x.at[p, k, s], recv_sem=rs_x.at[p, own[p], s],
            device_id=(((x + k) % NX) * NZ + z, col), device_id_type=MESH,
        )

    def e_args():
        return (embed_ref, etr, ss_e, rs_e, y * NZ + z, x * NC + core, on_diag)

    def ez_args(k):
        return (etr, ebuf.at[spot], ss_ez.at[k], rs_ez.at[spot], x * NZ + k, y * NC + half, z == k)

    def r_args(k):
        return (
            tile.at[1], srow.at[2 * quarter + core], ss_r.at[k], rs_r.at[2 * quarter + core],
            y * NZ + z, jnp.int32(k), jnp.logical_and(on_diag, col == k),
        )

    def f_args(k):
        return (fsrc, frcv.at[col], ss_f.at[k], rs_f.at[col], row, (col + k) % 8, never if k else col >= 0)

    def t_copy(k):
        return pltpu.make_async_remote_copy(
            src_ref=tot.at[quarter], dst_ref=tot.at[quarter], send_sem=ss_t.at[k], recv_sem=rs_t.at[quarter],
            device_id=(((x + k) % NX) * NZ + z, col), device_id_type=MESH,
        )

    def reduced(p):
        for k in range(8):
            arrived(a2a_rcv.at[p, k], rs_a.at[p, k])
        value = a2a_rcv[p, 0]
        for k in range(1, 8):
            value = value + a2a_rcv[p, k]
        return value

    def spread_z(p):
        for k in range(NZ):
            send(*z_args(p, k))

    def spread_x(p):
        for d in reversed(FAR):
            origin = (z + d) % NZ
            s = origin % 8

            @pl.when(origin // 8 == core)
            def _():
                for c in range(NC):
                    arrived(full.at[p, own[p], s, c], rs_z.at[p, s, c])
                for k in (2, 1, 3):
                    x_copy(p, k, s).start()

    def x_arrived(p, k):
        other = (own[p] + k) % NX
        for s in range(8):
            arrived(full.at[p, other, s], rs_x.at[p, other, s])

    def block(p, q):
        return jnp.concatenate([full[p, q, s].reshape(16, 128) for s in range(8)], axis=1)

    def columns(p):
        return jnp.concatenate([full[p, :, s].reshape(NEW, 128) for s in range(8)], axis=1)

    for k in (2, 1, 3, 0):
        for h in range(NC):
            send(*a2a_args(0, k, h))
    send(*e_args())

    pair = dot_t(appended, appended)
    diagonal = jnp.where(eye, pair, 0.0)
    sq_row = jnp.sum(diagonal, axis=0, keepdims=True)
    sq_col = jnp.sum(diagonal, axis=1, keepdims=True)
    gsrc[:, 0:NEW] = sq_row + sq_col - 2.0 * pair
    gsrc[:, NEW:] = jnp.zeros((NEW, NEW), jnp.float32)

    tile[0] = matern(reduced(0)) * (1.0 / (18.0 * NOBS))
    pl.semaphore_wait(ready, 2)
    spread_z(0)
    for k in range(2):
        send(*g_args(k))

    arrived(etr, rs_e)

    @pl.when(home)
    def _():
        for k in range(NZ):
            send(*ez_args(k))

    gram[...] = jnp.zeros((16, 128), jnp.float32)

    @pl.when(col < 2)
    def _():
        for k in range(8):
            arrived(grcv.at[k], rs_g.at[k])
        value = grcv[0]
        for k in range(1, 8):
            value = value + grcv[k]
        gram[pl.ds(pl.multiple_of(8 * (col % 2), 8), 8), 0:NEW] = matern(value[:, 0:NEW]) * (1.0 / NEW)

    cand_embed = jnp.broadcast_to(cand_embed_ref[...], (8, cand_ref.shape[0]))
    new_embed = jnp.dot(cand_embed, onehot, precision=HIGH, preferred_element_type=jnp.float32)[0:1]
    new_embed = jnp.sum(jnp.where(eye, new_embed, 0.0), axis=1, keepdims=True)
    inv_copy.wait()
    whole_hi, whole_lo = split(inv[...])
    inv_hi[...] = whole_hi
    inv_lo[...] = whole_lo

    spread_x(0)
    for k in (0, 1, 3, 2):
        if k:
            x_arrived(0, k)
        q = (x + k) % NX
        value = block(0, q)
        hi, lo = split(value)
        both = dot_t(jnp.concatenate([hi, lo], axis=0), inv_hi[...])
        a2a_src[1, pl.ds(pl.multiple_of(16 * q, 8), 16)] = both[0:16] + both[16:32] + dot_t(hi, inv_lo[...])
        for h in range(NC):
            send(*a2a_args(1, k, h))
    kernel_hi, kernel_lo = split(columns(0))
    for s in range(8):
        arrived(ebuf.at[s], rs_ez.at[s])
    embed = jnp.concatenate([ebuf[s] for s in range(8)], axis=1)
    tile[1] = reduced(1)
    spread_z(1)
    for k in range(8):
        send(*r_args(k))
    spread_x(1)
    solved = block(1, quarter)
    hi, lo = split(solved)
    both = dot_t(jnp.concatenate([hi, lo], axis=0), kernel_hi)
    fsrc[:, 0:NEW] = gram[:, 0:NEW] - (both[0:16] + both[16:32] + dot_t(hi, kernel_lo))
    fsrc[:, NEW:] = jnp.broadcast_to(jnp.sum(solved * embed, axis=1, keepdims=True), (16, NEW))
    for k in (4, 3, 5, 2, 6, 1, 7, 0):
        send(*f_args(k))
    for k in range(8):
        arrived(srow.at[k], rs_r.at[k])
    srows[...] = srow[...].reshape(NEW, 128)
    rows_out = pltpu.make_async_copy(srows, solved_rows_ref, out_sem.at[0])
    rows_out.start()
    for k in range(8):
        arrived(frcv.at[k], rs_f.at[k])
    total = frcv[0]
    for k in range(1, 8):
        total = total + frcv[k]
    tot[quarter] = total
    for k in (2, 1, 3):
        t_copy(k).start()
    for k in (1, 3, 2):
        x_arrived(1, k)
    scols[...] = columns(1)
    cols_out = pltpu.make_async_copy(scols, solved_cols_ref, out_sem.at[1])
    cols_out.start()
    for k in (1, 3, 2):
        other = (quarter + k) % NX
        arrived(tot.at[other], rs_t.at[other])
    total = tot[...].reshape(NEW, 128)
    total_ref[:, 0:NEW] = total[:, 0:NEW]
    total_ref[:, NEW:] = total[:, NEW:] * (1.0 / NOBS) - new_embed

    rows_out.wait()
    cols_out.wait()
    wait_sent(*e_args())
    for p in range(2):
        for k in range(NX):
            for h in range(NC):
                wait_sent(*a2a_args(p, k, h))
        for k in range(NZ):
            wait_sent(*z_args(p, k))
        for k in (1, 2, 3):
            for s in range(8):
                x_copy(p, k, s).wait_send()
    for k in (1, 2, 3):
        t_copy(k).wait_send()
    for k in range(2):
        wait_sent(*g_args(k))
    for k in range(8):
        wait_sent(*r_args(k))
        wait_sent(*f_args(k))

    @pl.when(home)
    def _():
        for k in range(NZ):
            wait_sent(*ez_args(k))


def finish_kernel(
    total_ref, solved_cols_hbm, solved_rows_hbm, update_ref, inverse_ref, weights_ref, shift_ref,
    solved_cols_ref, solved_rows_ref, sem,
):
    cols_in = pltpu.make_async_copy(solved_cols_hbm, solved_cols_ref, sem.at[0])
    rows_in = pltpu.make_async_copy(solved_rows_hbm, solved_rows_ref, sem.at[1])
    rows_in.start()
    cols_in.start()
    total = total_ref[...]
    sub = lax.broadcasted_iota(jnp.int32, (NEW, NEW), 0)
    lane = lax.broadcasted_iota(jnp.int32, (NEW, NEW), 1)
    eye = sub == lane
    matrix = total[:, 0:NEW] + jnp.where(eye, 1.0, 0.0)
    quad = total[:, NEW:NEW + 1]
    for base in range(0, NEW, GROUP):
        columns = [jnp.broadcast_to(matrix[:, k:k + 1], (NEW, NEW)) for k in range(base, base + GROUP)]
        for t in range(GROUP):
            k = base + t
            here = columns[t]
            pivot = here[k:k + 1, :]
            scale = jnp.where(pivot > 0.0, 1.0 / pivot, jnp.nan)
            at_lane, at_sub = lane == k, sub == k
            pivot_row = jnp.where(at_lane[0:1], 1.0, matrix[k:k + 1, :]) * scale
            matrix = jnp.where(at_sub, pivot_row, jnp.where(at_lane, 0.0, matrix) - here * pivot_row)
            for u in range(t + 1, GROUP):
                factor = columns[u][k:k + 1, :] * scale
                columns[u] = jnp.where(at_sub, factor, columns[u] - here * factor)
    inverse_ref[...] = matrix
    weights = jnp.sum(matrix * quad, axis=0, keepdims=True)
    weights_ref[...] = weights
    rows_in.wait()
    cols_in.wait()
    solved_rows = solved_rows_ref[...]
    shift_ref[...] = jnp.dot(
        jnp.broadcast_to(weights, (8, NEW)), solved_rows, precision=HIGH, preferred_element_type=jnp.float32
    )[0:1]
    left = jnp.dot(matrix, solved_rows, precision=HIGH, preferred_element_type=jnp.float32)
    left_hi, left_lo = split(left)
    cols_hi, cols_lo = split(solved_cols_ref[...])
    update_ref[...] = lax.dot_general(
        jnp.concatenate([left_hi, left_hi, left_lo], axis=0),
        jnp.concatenate([cols_hi, cols_lo, cols_hi], axis=0),
        (((0,), (0,)), ((), ())), preferred_element_type=jnp.float32,
    )


def on_device(inverse_kernel, points, candidates, obs_embed, cand_embed, chosen):
    rows, cols = inverse_kernel.shape
    f32 = jnp.float32
    vmem = pl.BlockSpec(memory_space=pltpu.VMEM)
    dma = pltpu.SemaphoreType.DMA
    total, solved_cols, solved_rows = pl.pallas_call(
        exchange_kernel,
        out_shape=(
            jax.ShapeDtypeStruct((NEW, 128), f32),
            jax.ShapeDtypeStruct((NEW, cols), f32),
            jax.ShapeDtypeStruct((NEW, rows), f32),
        ),
        in_specs=[pl.BlockSpec(memory_space=pl.ANY)] * 6,
        out_specs=(vmem, pl.BlockSpec(memory_space=pl.ANY), pl.BlockSpec(memory_space=pl.ANY)),
        scratch_shapes=[
            pltpu.VMEM((rows, cols), f32),
            pltpu.VMEM((rows, cols), jnp.bfloat16),
            pltpu.VMEM((rows, cols), jnp.bfloat16),
            pltpu.VMEM((2, NEW, 128), f32),
            pltpu.VMEM((2, 8, 8, 128), f32),
            pltpu.VMEM((2, 8, 128), f32),
            pltpu.VMEM((2, NX, 8, NC, 8, 128), f32),
            pltpu.VMEM((NEW, 128), f32),
            pltpu.VMEM((8, 8, 128), f32),
            pltpu.VMEM((16, 128), f32),
            pltpu.VMEM((1, 128), f32),
            pltpu.VMEM((8, 1, 128), f32),
            pltpu.VMEM((8, 8, 128), f32),
            pltpu.VMEM((16, 128), f32),
            pltpu.VMEM((8, 16, 128), f32),
            pltpu.VMEM((NX, 16, 128), f32),
            dma((2, NX, NC)), dma((2, 8)),
            dma((2, NZ)), dma((2, 8, NC)),
            dma((2, NX, 8)), dma((2, NX, 8)),
            dma((2,)), dma((8,)),
            dma((8,)), dma((8,)),
            dma((8,)), dma((8,)),
            dma((NX,)), dma((NX,)),
            dma, dma,
            dma((NZ,)), dma((8,)),
            dma,
            dma((2,)),
            pltpu.VMEM((NEW, cols), f32),
            pltpu.VMEM((NEW, rows), f32),
            pltpu.SemaphoreType.REGULAR,
            pltpu.VMEM(points.shape, points.dtype),
            pltpu.VMEM(candidates.shape, candidates.dtype),
            pltpu.VMEM((1, rows), f32),
            pltpu.VMEM((1, NEW), jnp.int32),
            pltpu.VMEM((1, cand_embed.shape[0]), f32),
            dma((5,)),
        ],
        compiler_params=pltpu.CompilerParams(collective_id=0, has_side_effects=True),
    )(inverse_kernel, points, candidates, obs_embed.reshape(1, rows),
      chosen.reshape(1, NEW), cand_embed.reshape(1, -1))
    update, inverse, weights, shift = pl.pallas_call(
        finish_kernel,
        out_shape=(
            jax.ShapeDtypeStruct((rows, cols), f32),
            jax.ShapeDtypeStruct((NEW, NEW), f32),
            jax.ShapeDtypeStruct((1, NEW), f32),
            jax.ShapeDtypeStruct((1, rows), f32),
        ),
        in_specs=[vmem] + [pl.BlockSpec(memory_space=pl.ANY)] * 2,
        out_specs=(vmem,) * 4,
        scratch_shapes=[pltpu.VMEM((NEW, cols), f32), pltpu.VMEM((NEW, rows), f32), dma((2,))],
    )(total, solved_cols, solved_rows)
    return update, inverse, weights.reshape(NEW), shift.reshape(rows)


def solution(mesh):
    return jax.shard_map(
        on_device,
        mesh=mesh,
        in_specs=(P("row", "col"), P("row", "col"), P(None, "col"), P("row"), P(), P()),
        out_specs=(P("row", "col"), P(), P(), P("row")),
        check_vma=False,
    )
```

```python
import jax
import jax.numpy as jnp
from jax import lax
from jax.experimental import pallas as pl
from jax.experimental.pallas import tpu as pltpu
from jax.sharding import PartitionSpec as P

MESH = pl.DeviceIdType.MESH
HIGH = lax.Precision.HIGHEST
NX, NY, NZ, NC = 4, 4, 16, 2
NOBS = 8192
NEW = 64
FAR = (8, 7, -7, 6, -6, 5, -5, 4, -4, 3, -3, 2, -2, 1, -1, 0)
GROUP = 8


def matern(square):
    scaled = jnp.sqrt(5.0 * jnp.maximum(square, 0.0))
    return (1.0 + scaled + scaled * scaled / 3.0) * jnp.exp(-scaled)


def dot_t(a, b, precision=None):
    return lax.dot_general(
        a, b, (((1,), (1,)), ((), ())), precision=precision, preferred_element_type=jnp.float32
    )


def split(value):
    hi = value.astype(jnp.bfloat16)
    return hi, (value - hi.astype(jnp.float32)).astype(jnp.bfloat16)


def exchange_kernel(
    inv_hbm, points_hbm, cand_hbm, embed_hbm, chosen_hbm, cand_embed_hbm,
    total_ref, solved_cols_ref, solved_rows_ref,
    inv, inv_hi, inv_lo, a2a_src, a2a_rcv, tile, full, gsrc, grcv, gram, etr, ebuf, srow, fsrc, frcv, tot,
    ss_a, rs_a, ss_z, rs_z, ss_x, rs_x, ss_g, rs_g, ss_r, rs_r, ss_f, rs_f, ss_t, rs_t, ss_e, rs_e, ss_ez, rs_ez, inv_sem, out_sem, scols, srows, ready,
    points_ref, cand_ref, embed_ref, chosen_ref, cand_embed_ref, in_sem,
):
    row = lax.axis_index("row")
    col = lax.axis_index("col")
    x, z = row // NZ, row % NZ
    y, core = col // NC, col % NC
    half = z // 8
    spot = z % 8
    mine = 2 * x + core
    quarter = (x + 2) % NX
    own = (x, quarter)
    on_diag = x == y
    home = core == half

    def send(src, dst, ssem, rsem, to_row, to_col, is_self):
        remote = pltpu.make_async_remote_copy(
            src_ref=src, dst_ref=dst, send_sem=ssem, recv_sem=rsem,
            device_id=(to_row, to_col), device_id_type=MESH,
        )

        @pl.when(is_self)
        def _():
            pltpu.make_async_copy(src, dst, rsem).start()

        @pl.when(jnp.logical_not(is_self))
        def _():
            remote.start()

    def wait_sent(src, dst, ssem, rsem, to_row, to_col, is_self):
        @pl.when(jnp.logical_not(is_self))
        def _():
            pltpu.make_async_remote_copy(
                src_ref=src, dst_ref=dst, send_sem=ssem, recv_sem=rsem,
                device_id=(to_row, to_col), device_id_type=MESH,
            ).wait_send()

    def arrived(dst, rsem):
        pltpu.make_async_copy(dst, dst, rsem).wait()

    loads = [
        pltpu.make_async_copy(src, dst, in_sem.at[k])
        for k, (src, dst) in enumerate((
            (chosen_hbm, chosen_ref), (cand_hbm, cand_ref), (points_hbm, points_ref),
            (embed_hbm, embed_ref), (cand_embed_hbm, cand_embed_ref),
        ))
    ]
    for load in loads:
        load.start()
    inv_copy = pltpu.make_async_copy(inv_hbm, inv, inv_sem)
    inv_copy.start()

    barrier = pltpu.get_barrier_semaphore()

    def greet(to_row, to_col, is_self):
        @pl.when(jnp.logical_not(is_self))
        def _():
            pl.semaphore_signal(barrier, inc=1, device_id=(to_row, to_col), device_id_type=MESH)

    for d in (4, -4, 3, -3, 2, -2, 1, -1):
        for h in range(NC):
            greet(x * NZ + (z + d) % NZ, y * NC + h, x < 0)
    for k in range(8):
        greet(y * NZ + z, jnp.int32(k), jnp.logical_and(on_diag, col == k))
        greet((k // 2) * NZ + z, x * NC + k % 2, jnp.logical_and(on_diag, mine == k))
        greet(row, jnp.int32(k), col == k)
    for k in range(4):
        greet(k * NZ + z, col, x == k)

    for load in loads:
        load.wait()
    eye = lax.broadcasted_iota(jnp.int32, (NEW, NEW), 0) == lax.broadcasted_iota(jnp.int32, (NEW, NEW), 1)
    index = jnp.sum(jnp.where(eye, chosen_ref[...].astype(jnp.float32), 0.0), axis=1, keepdims=True)
    picked = index == lax.broadcasted_iota(jnp.int32, (NEW, cand_ref.shape[0]), 1).astype(jnp.float32)
    appended = jnp.dot(
        jnp.where(picked, 1.0, 0.0).astype(jnp.bfloat16), cand_ref[...], preferred_element_type=jnp.float32
    ).astype(jnp.bfloat16)
    pts = points_ref[...]
    wide = pts.astype(jnp.float32)
    ones = jnp.ones((8, wide.shape[1]), jnp.bfloat16)
    sq_hi, sq_lo = split(wide * wide)
    sq_obs = (dot_t(ones, sq_hi) + dot_t(ones, sq_lo))[0:1]
    new = appended.astype(jnp.float32)
    sq_col = jnp.sum(new * new, axis=1, keepdims=True)
    a2a_src[0] = sq_obs + sq_col - 2.0 * dot_t(appended, pts)

    pl.semaphore_wait(barrier, 42 - 2 * on_diag.astype(jnp.int32))
    for d in (4, -4):
        pl.semaphore_signal(ready, inc=1, device_id=(x * NZ + (z + d) % NZ, col), device_id_type=MESH)

    never = x < 0

    def a2a_args(p, k, h):
        q = (x + k) % NX
        src = a2a_src.at[p, pl.ds(pl.multiple_of(16 * q + 8 * h, 8), 8)]
        is_self = jnp.logical_and(on_diag, core == h) if (k + 2 * p) % NX == 0 else never
        return (
            src, a2a_rcv.at[p, col], ss_a.at[p, k, h], rs_a.at[p, col],
            ((x + k + 2 * p) % NX) * NZ + z, x * NC + h, is_self,
        )

    def g_args(k):
        src = gsrc.at[pl.ds(pl.multiple_of(16 * quarter + 8 * k, 8), 8)]
        return (src, grcv.at[col], ss_g.at[k], rs_g.at[col], row, jnp.int32(k), col == k)

    def z_args(p, k):
        return (
            tile.at[p], full.at[p, own[p], spot, core], ss_z.at[p, k], rs_z.at[p, spot, core],
            x * NZ + (z + FAR[k]) % NZ, y * NC + half, jnp.logical_and(home, FAR[k] == 0),
        )

    def x_copy(p, k, s):
        return pltpu.make_async_remote_copy(
            src_ref=full.at[p, own[p], s], dst_ref=full.at[p, own[p], s],
            send_sem=ss_x.at[p, k, s], recv_sem=rs_x.at[p, own[p], s],
            device_id=(((x + k) % NX) * NZ + z, col), device_id_type=MESH,
        )

    def e_args():
        return (embed_ref, etr, ss_e, rs_e, y * NZ + z, x * NC + core, on_diag)

    def ez_args(k):
        return (etr, ebuf.at[spot], ss_ez.at[k], rs_ez.at[spot], x * NZ + k, y * NC + half, z == k)

    def r_args(k):
        return (
            tile.at[1], srow.at[2 * quarter + core], ss_r.at[k], rs_r.at[2 * quarter + core],
            y * NZ + z, jnp.int32(k), jnp.logical_and(on_diag, col == k),
        )

    def f_args(k):
        return (fsrc, frcv.at[col], ss_f.at[k], rs_f.at[col], row, (col + k) % 8, never if k else col >= 0)

    def t_copy(k):
        return pltpu.make_async_remote_copy(
            src_ref=tot.at[quarter], dst_ref=tot.at[quarter], send_sem=ss_t.at[k], recv_sem=rs_t.at[quarter],
            device_id=(((x + k) % NX) * NZ + z, col), device_id_type=MESH,
        )

    def reduced(p):
        for k in range(8):
            arrived(a2a_rcv.at[p, k], rs_a.at[p, k])
        value = a2a_rcv[p, 0]
        for k in range(1, 8):
            value = value + a2a_rcv[p, k]
        return value

    def spread_z(p):
        for k in range(NZ):
            send(*z_args(p, k))

    def spread_x(p):
        for d in reversed(FAR):
            origin = (z + d) % NZ
            s = origin % 8

            @pl.when(origin // 8 == core)
            def _():
                for c in range(NC):
                    arrived(full.at[p, own[p], s, c], rs_z.at[p, s, c])
                for k in (2, 1, 3):
                    x_copy(p, k, s).start()

    def x_arrived(p, k):
        other = (own[p] + k) % NX
        for s in range(8):
            arrived(full.at[p, other, s], rs_x.at[p, other, s])

    def block(p, q):
        return jnp.concatenate([full[p, q, s].reshape(16, 128) for s in range(8)], axis=1)

    def columns(p):
        return jnp.concatenate([full[p, :, s].reshape(NEW, 128) for s in range(8)], axis=1)

    for k in (2, 1, 3, 0):
        for h in range(NC):
            send(*a2a_args(0, k, h))
    send(*e_args())

    pair = dot_t(appended, appended)
    diagonal = jnp.where(eye, pair, 0.0)
    sq_row = jnp.sum(diagonal, axis=0, keepdims=True)
    sq_col = jnp.sum(diagonal, axis=1, keepdims=True)
    gsrc[:, 0:NEW] = sq_row + sq_col - 2.0 * pair
    gsrc[:, NEW:] = jnp.zeros((NEW, NEW), jnp.float32)

    tile[0] = matern(reduced(0)) * (1.0 / (18.0 * NOBS))
    pl.semaphore_wait(ready, 2)
    spread_z(0)
    for k in range(2):
        send(*g_args(k))

    arrived(etr, rs_e)

    @pl.when(home)
    def _():
        for k in range(NZ):
            send(*ez_args(k))

    gram[...] = jnp.zeros((16, 128), jnp.float32)

    @pl.when(col < 2)
    def _():
        for k in range(8):
            arrived(grcv.at[k], rs_g.at[k])
        value = grcv[0]
        for k in range(1, 8):
            value = value + grcv[k]
        gram[pl.ds(pl.multiple_of(8 * (col % 2), 8), 8), 0:NEW] = matern(value[:, 0:NEW]) * (1.0 / NEW)

    new_embed = jnp.sum(jnp.where(picked, cand_embed_ref[...], 0.0), axis=1, keepdims=True)
    inv_copy.wait()
    whole_hi, whole_lo = split(inv[...])
    inv_hi[...] = whole_hi
    inv_lo[...] = whole_lo

    spread_x(0)
    for k in (0, 1, 3, 2):
        if k:
            x_arrived(0, k)
        q = (x + k) % NX
        value = block(0, q)
        hi, lo = split(value)
        both = dot_t(jnp.concatenate([hi, lo], axis=0), inv_hi[...])
        a2a_src[1, pl.ds(pl.multiple_of(16 * q, 8), 16)] = both[0:16] + both[16:32] + dot_t(hi, inv_lo[...])
        for h in range(NC):
            send(*a2a_args(1, k, h))
    kernel_hi, kernel_lo = split(columns(0))
    for s in range(8):
        arrived(ebuf.at[s], rs_ez.at[s])
    embed = jnp.concatenate([ebuf[s] for s in range(8)], axis=1)
    tile[1] = reduced(1)
    spread_z(1)
    for k in range(8):
        send(*r_args(k))
    spread_x(1)
    solved = block(1, quarter)
    hi, lo = split(solved)
    both = dot_t(jnp.concatenate([hi, lo], axis=0), kernel_hi)
    fsrc[:, 0:NEW] = gram[:, 0:NEW] - (both[0:16] + both[16:32] + dot_t(hi, kernel_lo))
    fsrc[:, NEW:] = jnp.broadcast_to(jnp.sum(solved * embed, axis=1, keepdims=True), (16, NEW))
    for k in (4, 3, 5, 2, 6, 1, 7, 0):
        send(*f_args(k))
    for k in range(8):
        arrived(srow.at[k], rs_r.at[k])
    srows[...] = srow[...].reshape(NEW, 128)
    rows_out = pltpu.make_async_copy(srows, solved_rows_ref, out_sem.at[0])
    rows_out.start()
    for k in range(8):
        arrived(frcv.at[k], rs_f.at[k])
    total = frcv[0]
    for k in range(1, 8):
        total = total + frcv[k]
    tot[quarter] = total
    for k in (2, 1, 3):
        t_copy(k).start()
    for k in (1, 3, 2):
        x_arrived(1, k)
    scols[...] = columns(1)
    cols_out = pltpu.make_async_copy(scols, solved_cols_ref, out_sem.at[1])
    cols_out.start()
    for k in (1, 3, 2):
        other = (quarter + k) % NX
        arrived(tot.at[other], rs_t.at[other])
    total = tot[...].reshape(NEW, 128)
    total_ref[:, 0:NEW] = total[:, 0:NEW]
    total_ref[:, NEW:] = total[:, NEW:] * (1.0 / NOBS) - new_embed

    rows_out.wait()
    cols_out.wait()
    wait_sent(*e_args())
    for p in range(2):
        for k in range(NX):
            for h in range(NC):
                wait_sent(*a2a_args(p, k, h))
        for k in range(NZ):
            wait_sent(*z_args(p, k))
        for k in (1, 2, 3):
            for s in range(8):
                x_copy(p, k, s).wait_send()
    for k in (1, 2, 3):
        t_copy(k).wait_send()
    for k in range(2):
        wait_sent(*g_args(k))
    for k in range(8):
        wait_sent(*r_args(k))
        wait_sent(*f_args(k))

    @pl.when(home)
    def _():
        for k in range(NZ):
            wait_sent(*ez_args(k))


def finish_kernel(
    total_ref, solved_cols_hbm, solved_rows_hbm, update_ref, inverse_ref, weights_ref, shift_ref,
    solved_cols_ref, solved_rows_ref, sem,
):
    cols_in = pltpu.make_async_copy(solved_cols_hbm, solved_cols_ref, sem.at[0])
    rows_in = pltpu.make_async_copy(solved_rows_hbm, solved_rows_ref, sem.at[1])
    rows_in.start()
    cols_in.start()
    total = total_ref[...]
    sub = lax.broadcasted_iota(jnp.int32, (NEW, NEW), 0)
    lane = lax.broadcasted_iota(jnp.int32, (NEW, NEW), 1)
    eye = sub == lane
    matrix = total[:, 0:NEW] + jnp.where(eye, 1.0, 0.0)
    quad = total[:, NEW:NEW + 1]
    for base in range(0, NEW, GROUP):
        columns = [jnp.broadcast_to(matrix[:, k:k + 1], (NEW, NEW)) for k in range(base, base + GROUP)]
        for t in range(GROUP):
            k = base + t
            here = columns[t]
            pivot = here[k:k + 1, :]
            scale = jnp.where(pivot > 0.0, 1.0 / pivot, jnp.nan)
            at_lane, at_sub = lane == k, sub == k
            pivot_row = jnp.where(at_lane[0:1], 1.0, matrix[k:k + 1, :]) * scale
            matrix = jnp.where(at_sub, pivot_row, jnp.where(at_lane, 0.0, matrix) - here * pivot_row)
            for u in range(t + 1, GROUP):
                factor = columns[u][k:k + 1, :] * scale
                columns[u] = jnp.where(at_sub, factor, columns[u] - here * factor)
    inverse_ref[...] = matrix
    weights = jnp.sum(matrix * quad, axis=0, keepdims=True)
    weights_ref[...] = weights
    rows_in.wait()
    cols_in.wait()
    solved_rows = solved_rows_ref[...]
    shift_ref[...] = jnp.dot(
        jnp.broadcast_to(weights, (8, NEW)), solved_rows, precision=HIGH, preferred_element_type=jnp.float32
    )[0:1]
    left = jnp.dot(matrix, solved_rows, precision=HIGH, preferred_element_type=jnp.float32)
    left_hi, left_lo = split(left)
    cols_hi, cols_lo = split(solved_cols_ref[...])
    update_ref[...] = lax.dot_general(
        jnp.concatenate([left_hi, left_hi, left_lo], axis=0),
        jnp.concatenate([cols_hi, cols_lo, cols_hi], axis=0),
        (((0,), (0,)), ((), ())), preferred_element_type=jnp.float32,
    )


def on_device(inverse_kernel, points, candidates, obs_embed, cand_embed, chosen):
    rows, cols = inverse_kernel.shape
    f32 = jnp.float32
    vmem = pl.BlockSpec(memory_space=pltpu.VMEM)
    dma = pltpu.SemaphoreType.DMA
    total, solved_cols, solved_rows = pl.pallas_call(
        exchange_kernel,
        out_shape=(
            jax.ShapeDtypeStruct((NEW, 128), f32),
            jax.ShapeDtypeStruct((NEW, cols), f32),
            jax.ShapeDtypeStruct((NEW, rows), f32),
        ),
        in_specs=[pl.BlockSpec(memory_space=pl.ANY)] * 6,
        out_specs=(vmem, pl.BlockSpec(memory_space=pl.ANY), pl.BlockSpec(memory_space=pl.ANY)),
        scratch_shapes=[
            pltpu.VMEM((rows, cols), f32),
            pltpu.VMEM((rows, cols), jnp.bfloat16),
            pltpu.VMEM((rows, cols), jnp.bfloat16),
            pltpu.VMEM((2, NEW, 128), f32),
            pltpu.VMEM((2, 8, 8, 128), f32),
            pltpu.VMEM((2, 8, 128), f32),
            pltpu.VMEM((2, NX, 8, NC, 8, 128), f32),
            pltpu.VMEM((NEW, 128), f32),
            pltpu.VMEM((8, 8, 128), f32),
            pltpu.VMEM((16, 128), f32),
            pltpu.VMEM((1, 128), f32),
            pltpu.VMEM((8, 1, 128), f32),
            pltpu.VMEM((8, 8, 128), f32),
            pltpu.VMEM((16, 128), f32),
            pltpu.VMEM((8, 16, 128), f32),
            pltpu.VMEM((NX, 16, 128), f32),
            dma((2, NX, NC)), dma((2, 8)),
            dma((2, NZ)), dma((2, 8, NC)),
            dma((2, NX, 8)), dma((2, NX, 8)),
            dma((2,)), dma((8,)),
            dma((8,)), dma((8,)),
            dma((8,)), dma((8,)),
            dma((NX,)), dma((NX,)),
            dma, dma,
            dma((NZ,)), dma((8,)),
            dma,
            dma((2,)),
            pltpu.VMEM((NEW, cols), f32),
            pltpu.VMEM((NEW, rows), f32),
            pltpu.SemaphoreType.REGULAR,
            pltpu.VMEM(points.shape, points.dtype),
            pltpu.VMEM(candidates.shape, candidates.dtype),
            pltpu.VMEM((1, rows), f32),
            pltpu.VMEM((1, NEW), jnp.int32),
            pltpu.VMEM((1, cand_embed.shape[0]), f32),
            dma((5,)),
        ],
        compiler_params=pltpu.CompilerParams(collective_id=0, has_side_effects=True),
    )(inverse_kernel, points, candidates, obs_embed.reshape(1, rows),
      chosen.reshape(1, NEW), cand_embed.reshape(1, -1))
    update, inverse, weights, shift = pl.pallas_call(
        finish_kernel,
        out_shape=(
            jax.ShapeDtypeStruct((rows, cols), f32),
            jax.ShapeDtypeStruct((NEW, NEW), f32),
            jax.ShapeDtypeStruct((1, NEW), f32),
            jax.ShapeDtypeStruct((1, rows), f32),
        ),
        in_specs=[vmem] + [pl.BlockSpec(memory_space=pl.ANY)] * 2,
        out_specs=(vmem,) * 4,
        scratch_shapes=[pltpu.VMEM((NEW, cols), f32), pltpu.VMEM((NEW, rows), f32), dma((2,))],
    )(total, solved_cols, solved_rows)
    return update, inverse, weights.reshape(NEW), shift.reshape(rows)


def solution(mesh):
    return jax.shard_map(
        on_device,
        mesh=mesh,
        in_specs=(P("row", "col"), P("row", "col"), P(None, "col"), P("row"), P(), P()),
        out_specs=(P("row", "col"), P(), P(), P("row")),
        check_vma=False,
    )
```

```python
import jax
import jax.numpy as jnp
from jax import lax
from jax.experimental import pallas as pl
from jax.experimental.pallas import tpu as pltpu
from jax.sharding import PartitionSpec as P

MESH = pl.DeviceIdType.MESH
HIGH = lax.Precision.HIGHEST
NX, NY, NZ, NC = 4, 4, 16, 2
NOBS = 8192
NEW = 64
FAR = (8, 7, -7, 6, -6, 5, -5, 4, -4, 3, -3, 2, -2, 1, -1, 0)
GROUP = 8


def matern(square):
    scaled = jnp.sqrt(5.0 * jnp.maximum(square, 0.0))
    return (1.0 + scaled + scaled * scaled / 3.0) * jnp.exp(-scaled)


def dot_t(a, b, precision=None):
    return lax.dot_general(
        a, b, (((1,), (1,)), ((), ())), precision=precision, preferred_element_type=jnp.float32
    )


def split(value):
    hi = value.astype(jnp.bfloat16)
    return hi, (value - hi.astype(jnp.float32)).astype(jnp.bfloat16)


def exchange_kernel(
    inv_hbm, points_hbm, cand_hbm, embed_hbm, chosen_hbm, cand_embed_hbm,
    total_ref, solved_cols_ref, solved_rows_ref,
    inv, inv_hi, inv_lo, a2a_src, a2a_rcv, tile, full, gsrc, grcv, gram, etr, ebuf, srow, fsrc, frcv, tot,
    ss_a, rs_a, ss_z, rs_z, ss_x, rs_x, ss_g, rs_g, ss_r, rs_r, ss_f, rs_f, ss_t, rs_t, ss_e, rs_e, ss_ez, rs_ez, inv_sem, out_sem, scols, srows, ready,
    points_ref, cand_ref, embed_ref, chosen_ref, cand_embed_ref, in_sem,
):
    row = lax.axis_index("row")
    col = lax.axis_index("col")
    x, z = row // NZ, row % NZ
    y, core = col // NC, col % NC
    half = z // 8
    spot = z % 8
    mine = 2 * x + core
    quarter = (x + 2) % NX
    own = (x, quarter)
    on_diag = x == y
    home = core == half

    def send(src, dst, ssem, rsem, to_row, to_col, is_self):
        remote = pltpu.make_async_remote_copy(
            src_ref=src, dst_ref=dst, send_sem=ssem, recv_sem=rsem,
            device_id=(to_row, to_col), device_id_type=MESH,
        )

        @pl.when(is_self)
        def _():
            pltpu.make_async_copy(src, dst, rsem).start()

        @pl.when(jnp.logical_not(is_self))
        def _():
            remote.start()

    def wait_sent(src, dst, ssem, rsem, to_row, to_col, is_self):
        @pl.when(jnp.logical_not(is_self))
        def _():
            pltpu.make_async_remote_copy(
                src_ref=src, dst_ref=dst, send_sem=ssem, recv_sem=rsem,
                device_id=(to_row, to_col), device_id_type=MESH,
            ).wait_send()

    def arrived(dst, rsem):
        pltpu.make_async_copy(dst, dst, rsem).wait()

    loads = [
        pltpu.make_async_copy(src, dst, in_sem.at[k])
        for k, (src, dst) in enumerate((
            (chosen_hbm, chosen_ref), (cand_hbm, cand_ref), (points_hbm, points_ref),
            (embed_hbm, embed_ref), (cand_embed_hbm, cand_embed_ref),
        ))
    ]
    for load in loads:
        load.start()
    inv_copy = pltpu.make_async_copy(inv_hbm, inv, inv_sem)
    inv_copy.start()

    barrier = pltpu.get_barrier_semaphore()

    def greet(to_row, to_col, is_self):
        @pl.when(jnp.logical_not(is_self))
        def _():
            pl.semaphore_signal(barrier, inc=1, device_id=(to_row, to_col), device_id_type=MESH)

    for d in (4, -4, 3, -3, 2, -2, 1, -1):
        for h in range(NC):
            greet(x * NZ + (z + d) % NZ, y * NC + h, x < 0)
    for k in range(8):
        greet(y * NZ + z, jnp.int32(k), jnp.logical_and(on_diag, col == k))
        greet((k // 2) * NZ + z, x * NC + k % 2, jnp.logical_and(on_diag, mine == k))
        greet(row, jnp.int32(k), col == k)
    for k in range(4):
        greet(k * NZ + z, col, x == k)

    for load in loads:
        load.wait()
    eye = lax.broadcasted_iota(jnp.int32, (NEW, NEW), 0) == lax.broadcasted_iota(jnp.int32, (NEW, NEW), 1)
    index = jnp.sum(jnp.where(eye, chosen_ref[...].astype(jnp.float32), 0.0), axis=1, keepdims=True)
    picked = index == lax.broadcasted_iota(jnp.int32, (NEW, cand_ref.shape[0]), 1).astype(jnp.float32)
    appended = jnp.dot(
        jnp.where(picked, 1.0, 0.0).astype(jnp.bfloat16), cand_ref[...], preferred_element_type=jnp.float32
    ).astype(jnp.bfloat16)
    pts = points_ref[...]
    wide = pts.astype(jnp.float32)
    ones = jnp.ones((8, wide.shape[1]), jnp.bfloat16)
    sq_hi, sq_lo = split(wide * wide)
    sq_obs = (dot_t(ones, sq_hi) + dot_t(ones, sq_lo))[0:1]
    new = appended.astype(jnp.float32)
    sq_col = jnp.sum(new * new, axis=1, keepdims=True)
    a2a_src[0] = sq_obs + sq_col - 2.0 * dot_t(appended, pts)

    pl.semaphore_wait(barrier, 42 - 2 * on_diag.astype(jnp.int32))
    for d in (4, -4):
        pl.semaphore_signal(ready, inc=1, device_id=(x * NZ + (z + d) % NZ, col), device_id_type=MESH)

    never = x < 0

    def a2a_args(p, k, h):
        q = (x + k) % NX
        src = a2a_src.at[p, pl.ds(pl.multiple_of(16 * q + 8 * h, 8), 8)]
        is_self = jnp.logical_and(on_diag, core == h) if (k + 2 * p) % NX == 0 else never
        return (
            src, a2a_rcv.at[p, col], ss_a.at[p, k, h], rs_a.at[p, col],
            ((x + k + 2 * p) % NX) * NZ + z, x * NC + h, is_self,
        )

    def g_args(k):
        src = gsrc.at[pl.ds(pl.multiple_of(16 * quarter + 8 * k, 8), 8)]
        return (src, grcv.at[col], ss_g.at[k], rs_g.at[col], row, jnp.int32(k), col == k)

    def z_args(p, k):
        return (
            tile.at[p], full.at[p, own[p], spot, core], ss_z.at[p, k], rs_z.at[p, spot, core],
            x * NZ + (z + FAR[k]) % NZ, y * NC + half, jnp.logical_and(home, FAR[k] == 0),
        )

    def x_copy(p, k, s):
        return pltpu.make_async_remote_copy(
            src_ref=full.at[p, own[p], s], dst_ref=full.at[p, own[p], s],
            send_sem=ss_x.at[p, k, s], recv_sem=rs_x.at[p, own[p], s],
            device_id=(((x + k) % NX) * NZ + z, col), device_id_type=MESH,
        )

    def e_args():
        return (embed_ref, etr, ss_e, rs_e, y * NZ + z, x * NC + core, on_diag)

    def ez_args(k):
        return (etr, ebuf.at[spot], ss_ez.at[k], rs_ez.at[spot], x * NZ + k, y * NC + half, z == k)

    def r_args(k):
        return (
            tile.at[1], srow.at[2 * quarter + core], ss_r.at[k], rs_r.at[2 * quarter + core],
            y * NZ + z, jnp.int32(k), jnp.logical_and(on_diag, col == k),
        )

    def f_args(k):
        return (fsrc, frcv.at[col], ss_f.at[k], rs_f.at[col], row, (col + k) % 8, never if k else col >= 0)

    def t_copy(k):
        return pltpu.make_async_remote_copy(
            src_ref=tot.at[quarter], dst_ref=tot.at[quarter], send_sem=ss_t.at[k], recv_sem=rs_t.at[quarter],
            device_id=(((x + k) % NX) * NZ + z, col), device_id_type=MESH,
        )

    def reduced(p):
        for k in range(8):
            arrived(a2a_rcv.at[p, k], rs_a.at[p, k])
        value = a2a_rcv[p, 0]
        for k in range(1, 8):
            value = value + a2a_rcv[p, k]
        return value

    def spread_z(p):
        for k in range(NZ):
            send(*z_args(p, k))

    def spread_x(p):
        for d in reversed(FAR):
            origin = (z + d) % NZ
            s = origin % 8

            @pl.when(origin // 8 == core)
            def _():
                for c in range(NC):
                    arrived(full.at[p, own[p], s, c], rs_z.at[p, s, c])
                for k in (2, 1, 3):
                    x_copy(p, k, s).start()

    def x_arrived(p, k):
        other = (own[p] + k) % NX
        for s in range(8):
            arrived(full.at[p, other, s], rs_x.at[p, other, s])

    def block(p, q):
        return jnp.concatenate([full[p, q, s].reshape(16, 128) for s in range(8)], axis=1)

    def columns(p):
        return jnp.concatenate([full[p, :, s].reshape(NEW, 128) for s in range(8)], axis=1)

    for k in (2, 1, 3, 0):
        for h in range(NC):
            send(*a2a_args(0, k, h))
    send(*e_args())

    pair = dot_t(appended, appended)
    diagonal = jnp.where(eye, pair, 0.0)
    sq_row = jnp.sum(diagonal, axis=0, keepdims=True)
    sq_col = jnp.sum(diagonal, axis=1, keepdims=True)
    gsrc[:, 0:NEW] = sq_row + sq_col - 2.0 * pair
    gsrc[:, NEW:] = jnp.zeros((NEW, NEW), jnp.float32)

    tile[0] = matern(reduced(0)) * (1.0 / (18.0 * NOBS))
    pl.semaphore_wait(ready, 2)
    spread_z(0)
    for k in range(2):
        send(*g_args(k))

    arrived(etr, rs_e)

    @pl.when(home)
    def _():
        for k in range(NZ):
            send(*ez_args(k))

    gram[...] = jnp.zeros((16, 128), jnp.float32)

    @pl.when(col < 2)
    def _():
        for k in range(8):
            arrived(grcv.at[k], rs_g.at[k])
        value = grcv[0]
        for k in range(1, 8):
            value = value + grcv[k]
        gram[pl.ds(pl.multiple_of(8 * (col % 2), 8), 8), 0:NEW] = matern(value[:, 0:NEW]) * (1.0 / NEW)

    new_embed = jnp.sum(jnp.where(picked, cand_embed_ref[...], 0.0), axis=1, keepdims=True)
    inv_copy.wait()
    whole_hi, whole_lo = split(inv[...])
    inv_hi[...] = whole_hi
    inv_lo[...] = whole_lo

    spread_x(0)
    for k in (0, 1, 3, 2):
        if k:
            x_arrived(0, k)
        q = (x + k) % NX
        value = block(0, q)
        hi, lo = split(value)
        both = dot_t(jnp.concatenate([hi, lo], axis=0), inv_hi[...])
        a2a_src[1, pl.ds(pl.multiple_of(16 * q, 8), 16)] = both[0:16] + both[16:32] + dot_t(hi, inv_lo[...])
        for h in range(NC):
            send(*a2a_args(1, k, h))
    kernel_hi, kernel_lo = split(columns(0))
    for s in range(8):
        arrived(ebuf.at[s], rs_ez.at[s])
    embed = jnp.concatenate([ebuf[s] for s in range(8)], axis=1)
    tile[1] = reduced(1)
    spread_z(1)
    for k in range(8):
        send(*r_args(k))
    spread_x(1)
    solved = block(1, quarter)
    hi, lo = split(solved)
    both = dot_t(jnp.concatenate([hi, lo], axis=0), kernel_hi)
    fsrc[:, 0:NEW] = gram[:, 0:NEW] - (both[0:16] + both[16:32] + dot_t(hi, kernel_lo))
    fsrc[:, NEW:] = jnp.broadcast_to(jnp.sum(solved * embed, axis=1, keepdims=True), (16, NEW))
    for k in (4, 3, 5, 2, 6, 1, 7, 0):
        send(*f_args(k))
    for k in range(8):
        arrived(srow.at[k], rs_r.at[k])
    srows[...] = srow[...].reshape(NEW, 128)
    rows_out = pltpu.make_async_copy(srows, solved_rows_ref, out_sem.at[0])
    rows_out.start()
    for k in range(8):
        arrived(frcv.at[k], rs_f.at[k])
    total = frcv[0]
    for k in range(1, 8):
        total = total + frcv[k]
    tot[quarter] = total
    for k in (2, 1, 3):
        t_copy(k).start()
    for k in (1, 3, 2):
        x_arrived(1, k)
    scols[...] = columns(1)
    cols_out = pltpu.make_async_copy(scols, solved_cols_ref, out_sem.at[1])
    cols_out.start()
    for k in (1, 3, 2):
        other = (quarter + k) % NX
        arrived(tot.at[other], rs_t.at[other])
    total = tot[...].reshape(NEW, 128)
    total_ref[:, 0:NEW] = total[:, 0:NEW]
    total_ref[:, NEW:] = total[:, NEW:] * (1.0 / NOBS) - new_embed

    rows_out.wait()
    cols_out.wait()
    wait_sent(*e_args())
    for p in range(2):
        for k in range(NX):
            for h in range(NC):
                wait_sent(*a2a_args(p, k, h))
        for k in range(NZ):
            wait_sent(*z_args(p, k))
        for k in (1, 2, 3):
            for s in range(8):
                x_copy(p, k, s).wait_send()
    for k in (1, 2, 3):
        t_copy(k).wait_send()
    for k in range(2):
        wait_sent(*g_args(k))
    for k in range(8):
        wait_sent(*r_args(k))
        wait_sent(*f_args(k))

    @pl.when(home)
    def _():
        for k in range(NZ):
            wait_sent(*ez_args(k))


def finish_kernel(
    total_ref, solved_cols_hbm, solved_rows_hbm, update_hbm, inverse_ref, weights_ref, shift_ref,
    solved_cols_ref, solved_rows_ref, update_ref, sem,
):
    cols_in = pltpu.make_async_copy(solved_cols_hbm, solved_cols_ref, sem.at[0])
    rows_in = pltpu.make_async_copy(solved_rows_hbm, solved_rows_ref, sem.at[1])
    rows_in.start()
    cols_in.start()
    total = total_ref[...]
    sub = lax.broadcasted_iota(jnp.int32, (NEW, NEW), 0)
    lane = lax.broadcasted_iota(jnp.int32, (NEW, NEW), 1)
    eye = sub == lane
    matrix = total[:, 0:NEW] + jnp.where(eye, 1.0, 0.0)
    quad = total[:, NEW:NEW + 1]
    for base in range(0, NEW, GROUP):
        columns = [jnp.broadcast_to(matrix[:, k:k + 1], (NEW, NEW)) for k in range(base, base + GROUP)]
        for t in range(GROUP):
            k = base + t
            here = columns[t]
            pivot = here[k:k + 1, :]
            scale = jnp.where(pivot > 0.0, 1.0 / pivot, jnp.nan)
            at_lane, at_sub = lane == k, sub == k
            pivot_row = jnp.where(at_lane[0:1], 1.0, matrix[k:k + 1, :]) * scale
            matrix = jnp.where(at_sub, pivot_row, jnp.where(at_lane, 0.0, matrix) - here * pivot_row)
            for u in range(t + 1, GROUP):
                factor = columns[u][k:k + 1, :] * scale
                columns[u] = jnp.where(at_sub, factor, columns[u] - here * factor)
    inverse_ref[...] = matrix
    weights = jnp.sum(matrix * quad, axis=0, keepdims=True)
    weights_ref[...] = weights
    rows_in.wait()
    cols_in.wait()
    solved_rows = solved_rows_ref[...]
    shift_ref[...] = jnp.dot(
        jnp.broadcast_to(weights, (8, NEW)), solved_rows, precision=HIGH, preferred_element_type=jnp.float32
    )[0:1]
    left = jnp.dot(matrix, solved_rows, precision=HIGH, preferred_element_type=jnp.float32)
    left_hi, left_lo = split(left)
    cols_hi, cols_lo = split(solved_cols_ref[...])
    a = jnp.concatenate([left_hi, left_hi, left_lo], axis=0)
    b = jnp.concatenate([cols_hi, cols_lo, cols_hi], axis=0)
    copies = []
    for k in range(2):
        rows = pl.ds(64 * k, 64)
        update_ref[rows, :] = lax.dot_general(
            a[:, 64 * k:64 * k + 64], b, (((0,), (0,)), ((), ())), preferred_element_type=jnp.float32
        )
        copies.append(pltpu.make_async_copy(update_ref.at[rows], update_hbm.at[rows], sem.at[2 + k]))
        copies[k].start()
    for copy in copies:
        copy.wait()


def on_device(inverse_kernel, points, candidates, obs_embed, cand_embed, chosen):
    rows, cols = inverse_kernel.shape
    f32 = jnp.float32
    vmem = pl.BlockSpec(memory_space=pltpu.VMEM)
    dma = pltpu.SemaphoreType.DMA
    total, solved_cols, solved_rows = pl.pallas_call(
        exchange_kernel,
        out_shape=(
            jax.ShapeDtypeStruct((NEW, 128), f32),
            jax.ShapeDtypeStruct((NEW, cols), f32),
            jax.ShapeDtypeStruct((NEW, rows), f32),
        ),
        in_specs=[pl.BlockSpec(memory_space=pl.ANY)] * 6,
        out_specs=(vmem, pl.BlockSpec(memory_space=pl.ANY), pl.BlockSpec(memory_space=pl.ANY)),
        scratch_shapes=[
            pltpu.VMEM((rows, cols), f32),
            pltpu.VMEM((rows, cols), jnp.bfloat16),
            pltpu.VMEM((rows, cols), jnp.bfloat16),
            pltpu.VMEM((2, NEW, 128), f32),
            pltpu.VMEM((2, 8, 8, 128), f32),
            pltpu.VMEM((2, 8, 128), f32),
            pltpu.VMEM((2, NX, 8, NC, 8, 128), f32),
            pltpu.VMEM((NEW, 128), f32),
            pltpu.VMEM((8, 8, 128), f32),
            pltpu.VMEM((16, 128), f32),
            pltpu.VMEM((1, 128), f32),
            pltpu.VMEM((8, 1, 128), f32),
            pltpu.VMEM((8, 8, 128), f32),
            pltpu.VMEM((16, 128), f32),
            pltpu.VMEM((8, 16, 128), f32),
            pltpu.VMEM((NX, 16, 128), f32),
            dma((2, NX, NC)), dma((2, 8)),
            dma((2, NZ)), dma((2, 8, NC)),
            dma((2, NX, 8)), dma((2, NX, 8)),
            dma((2,)), dma((8,)),
            dma((8,)), dma((8,)),
            dma((8,)), dma((8,)),
            dma((NX,)), dma((NX,)),
            dma, dma,
            dma((NZ,)), dma((8,)),
            dma,
            dma((2,)),
            pltpu.VMEM((NEW, cols), f32),
            pltpu.VMEM((NEW, rows), f32),
            pltpu.SemaphoreType.REGULAR,
            pltpu.VMEM(points.shape, points.dtype),
            pltpu.VMEM(candidates.shape, candidates.dtype),
            pltpu.VMEM((1, rows), f32),
            pltpu.VMEM((1, NEW), jnp.int32),
            pltpu.VMEM((1, cand_embed.shape[0]), f32),
            dma((5,)),
        ],
        compiler_params=pltpu.CompilerParams(collective_id=0, has_side_effects=True),
    )(inverse_kernel, points, candidates, obs_embed.reshape(1, rows),
      chosen.reshape(1, NEW), cand_embed.reshape(1, -1))
    update, inverse, weights, shift = pl.pallas_call(
        finish_kernel,
        out_shape=(
            jax.ShapeDtypeStruct((rows, cols), f32),
            jax.ShapeDtypeStruct((NEW, NEW), f32),
            jax.ShapeDtypeStruct((1, NEW), f32),
            jax.ShapeDtypeStruct((1, rows), f32),
        ),
        in_specs=[vmem] + [pl.BlockSpec(memory_space=pl.ANY)] * 2,
        out_specs=(pl.BlockSpec(memory_space=pl.ANY), vmem, vmem, vmem),
        scratch_shapes=[pltpu.VMEM((NEW, cols), f32), pltpu.VMEM((NEW, rows), f32), pltpu.VMEM((rows, cols), f32), dma((4,))],
    )(total, solved_cols, solved_rows)
    return update, inverse, weights.reshape(NEW), shift.reshape(rows)


def solution(mesh):
    return jax.shard_map(
        on_device,
        mesh=mesh,
        in_specs=(P("row", "col"), P("row", "col"), P(None, "col"), P("row"), P(), P()),
        out_specs=(P("row", "col"), P(), P(), P("row")),
        check_vma=False,
    )
```
